32 devices in a mesh: row: 8 (over y, x, core), col: 4 (over z).
Axes of the slice: x: 2, y: 2, z: 4, core: 2. Of those that a mesh axis runs over, the one named last changes fastest.
Arguments:
- tokens: bfloat16 [1024, 2048], P('row', 'col'), may hold values from -6 to 6
- segment_ids: int32 [1024], replicated, may hold values from 0 to 15, never falling along the last dimension, each value on 1 to 128 neighbouring positions
- bucket_table: int32 [255], replicated, may hold values from 0 to 31
- slot_index: int32 [8, 1], P('row'), may hold values from 0 to 0, each once within a row
- gain_attn: float32 [2048], replicated, may hold values from 0.1 to 1.9
- w_qkv: bfloat16 [3, 2048, 2048], P(None, 'row', 'col'), may hold values from -0.09375 to 0.09375
- rel_bias: float32 [32, 32], P(None, 'col'), may hold values from -260 to 260
- w_out: bfloat16 [2048, 2048], P('col', 'row'), may hold values from -0.125 to 0.125
- gain_ffn: float32 [2048], replicated, may hold values from 0.1 to 1.9
- w_in: bfloat16 [2, 2048, 5120], P(None, 'row', 'col'), may hold values from -0.125 to 0.125
- w_down: bfloat16 [5120, 2048], P('col', 'row'), may hold values from -0.078125 to 0.078125
Outputs:
- output: bfloat16 [1024, 2048], P('row', 'col')
- kv_cache: bfloat16 [2, 1024, 2048], P(None, 'row', 'col')
The draws below stay inside these ranges and needn't reach their ends.
Inputs may be any that keep to these rules, and one draw needn't show every extreme that they name: `segment_ids`: segment numbers never fall along the tokens; each prompt spans 1 to 128 tokens and one spans exactly 128. `slot_index`: each row names each of 0 to 0 once.
All inputs are finite; a program needn't handle non-finite values.
Results may differ from the reference program's by a relative error of at most 0.009.
Values may be sent and summed in bfloat16 or wider, within the bound.
No kernel may reach another device: no remote copies, remote signals or barrier semaphores. Data moves between devices by JAX's collectives and lax.ppermute only.
A program may use at most 128 MiB of HBM per device.

```python
import math
import jax
import jax.numpy as jnp
import numpy as np
from jax import lax

D = 2048
HEADS = 32
HEAD_DIM = 64
FF = 5120
BUCKETS = 32
TOK_ROW = 128
BLOCK = 128
INNER = 2048
TOKENS = 1024
SEGS = 16
BLK_DEV = 1
N_ROW = 8


def draw_rel_bias(key, part):
    base = jax.random.normal(key, (BUCKETS, HEADS), jnp.float32)
    return base


def place_ends(values, key, least, top_value):
    longest = values.shape.index(max(values.shape))
    spots = []
    for shift in (0, 1):
        where = [jax.random.randint(jax.random.fold_in(key, axis), (), 0, length) for axis, length in enumerate(values.shape)]
        where[longest] = (where[longest] + shift) % values.shape[longest]
        spots.append(tuple(where))
    return values.at[spots[0]].set(least).at[spots[1]].set(top_value)


def levels(own_key, dims, pieces, low, largest):
    def one(position, blocks):
        heights = jax.random.uniform(jax.random.fold_in(jax.random.fold_in(own_key, 6), position), (blocks,), jnp.float32, low / len(pieces), largest / len(pieces))
        return jnp.repeat(jnp.exp(heights), dims[position] // blocks).reshape((-1,) + (1,) * (len(dims) - position - 1))

    gain = one(*pieces[0])
    for cut in pieces[1:]:
        gain = gain * one(*cut)
    return gain


def profile(number_of, total, most, lean):
    portions = [(1 << 20) // math.isqrt(standing ** lean) + 1 for standing in range(2, number_of + 1)]
    spare, given = total - most - (number_of - 1), [1] * (number_of - 1)
    while spare > 0:
        candidates = [i for i in range(number_of - 1) if given[i] < most]
        mass, left = sum([portions[i] for i in candidates]), spare
        for i in candidates:
            addition = min(most - given[i], max(1, left * portions[i] // mass), spare)
            given[i] = given[i] + addition
            spare = spare - addition
    return np.array([most] + given)


def uneven_parts(rng, count, total, limit, skew):
    if count == 2:
        one = jax.random.randint(rng, (), max(1, total - limit), min(limit, total - 1) + 1)
        return jnp.stack([one, total - one])
    sizes = jnp.asarray(profile(count, total, limit, skew), jnp.int32)
    twos = (count - 1) // 2
    donor, taker = sizes[1:1 + 2 * twos:2], sizes[2:2 + 2 * twos:2]
    margin = jnp.minimum(donor - 1, limit - taker)
    moved = jax.random.randint(jax.random.fold_in(rng, 1), (twos,), 0, 1 << 20) % (margin + 1)
    sizes = sizes.at[1:1 + 2 * twos:2].set(donor - moved).at[2:2 + 2 * twos:2].set(taker + moved)
    return sizes[jax.random.permutation(jax.random.fold_in(rng, 2), count)]


def scatter_about(own_key, extent, spread, most, split=(), kind=jnp.bfloat16):
    level = levels(own_key, extent, split, -0.22, 0.18) if split else 1.0
    array = jax.random.normal(own_key, extent, jnp.float32) * spread * level
    return jnp.minimum(jnp.maximum(array, -most), most).astype(kind)


def setup_inputs(seed: int = 0) -> dict:
    streams_of = jax.random.split(jax.random.key(seed), 12)
    return {
        "tokens": scatter_about(streams_of[0], (TOKENS, D), 1.0, 6.0, ((0, 8), (1, 4))),
        "segment_ids": jnp.searchsorted(jnp.cumsum(uneven_parts(streams_of[1], SEGS, TOKENS, TOK_ROW, 2)), jnp.arange(TOKENS), side="right").astype(jnp.int32),
        "bucket_table": place_ends(jax.random.randint(streams_of[2], (2 * TOK_ROW - 1,), 0, BUCKETS), jax.random.fold_in(streams_of[2], 1), 0, BUCKETS - 1).astype(jnp.int32),
        "slot_index": jax.vmap(lambda own: jax.random.permutation(own, BLK_DEV))(jax.random.split(streams_of[3], N_ROW)).reshape((N_ROW, BLK_DEV)).astype(jnp.int32),
        "gain_attn": jnp.clip(1.0 + 0.18 * jax.random.normal(streams_of[4], (D,), jnp.float32), 0.1, 1.9),
        "w_qkv": scatter_about(streams_of[5], (3, D, INNER), (2 * D) ** -0.5, 0.09375, ((1, 8), (2, 4))),
        "rel_bias": draw_rel_bias(jax.random.fold_in(streams_of[11], 71), 0),
        "w_out": scatter_about(streams_of[7], (INNER, D), INNER ** -0.5, 0.125, ((0, 4), (1, 8))),
        "gain_ffn": jnp.clip(1.0 + 0.18 * jax.random.normal(streams_of[8], (D,), jnp.float32), 0.1, 1.9),
        "w_in": scatter_about(streams_of[9], (2, D, FF), D ** -0.5, 0.125, ((1, 8), (2, 4))),
        "w_down": scatter_about(streams_of[10], (FF, D), FF ** -0.5, 0.078125, ((0, 4), (1, 8))),
    }


epsilon = 1e-06
masked_score = -1e+30

def rms_normed(values, gain_vector):
    widened = values.astype(jnp.float32)
    factor = lax.rsqrt(lax.optimization_barrier(jnp.mean(widened * widened, axis=1, keepdims=True)) + epsilon)
    return (widened * factor * gain_vector).astype(jnp.bfloat16)

def reference(tokens, segment_ids, bucket_table, slot_index, gain_attn, w_qkv, rel_bias, w_out, gain_ffn, w_in, w_down):
    normed = rms_normed(tokens, gain_attn)
    queries = lax.optimization_barrier(jnp.dot(normed, w_qkv[0], preferred_element_type=jnp.float32).astype(jnp.bfloat16))
    key_rows = lax.optimization_barrier(jnp.dot(normed, w_qkv[1], preferred_element_type=jnp.float32).astype(jnp.bfloat16))
    value_rows = lax.optimization_barrier(jnp.dot(normed, w_qkv[2], preferred_element_type=jnp.float32).astype(jnp.bfloat16))
    span = TOK_ROW
    key_padded = jnp.pad(key_rows, ((span, span), (0, 0)))
    value_padded = jnp.pad(value_rows, ((span, span), (0, 0)))
    seg_padded = jnp.pad(segment_ids, (span, span), constant_values=-1)
    bias_rows = jnp.take(rel_bias, bucket_table, axis=0).T

    def attend_block(index):
        start_row = index * span
        block_q = lax.dynamic_slice_in_dim(queries, start_row, span, 0).astype(jnp.float32).reshape(span, HEADS, HEAD_DIM)
        block_k = lax.dynamic_slice_in_dim(key_padded, start_row, 3 * span, 0).astype(jnp.float32).reshape(3 * span, HEADS, HEAD_DIM)
        block_v = lax.dynamic_slice_in_dim(value_padded, start_row, 3 * span, 0).astype(jnp.float32).reshape(3 * span, HEADS, HEAD_DIM)
        query_pos = start_row + jnp.arange(span, dtype=jnp.int32)
        key_pos = start_row - span + jnp.arange(3 * span, dtype=jnp.int32)
        query_seg = lax.dynamic_slice_in_dim(segment_ids, start_row, span, 0)
        key_seg = lax.dynamic_slice_in_dim(seg_padded, start_row, 3 * span, 0)
        allowed = query_seg[:, None] == key_seg[None, :]
        offset = jnp.clip(key_pos[None, :] - query_pos[:, None] + span - 1, 0, 2 * span - 2)
        scores = jnp.einsum('qhd,khd->hqk', block_q, block_k, precision=lax.Precision.HIGHEST)
        scores = scores + jnp.take(bias_rows, offset, axis=1)
        scores = jnp.where(allowed[None], scores, masked_score)
        top_score = lax.optimization_barrier(jnp.max(scores, axis=2, keepdims=True))
        weights = jnp.where(allowed[None], jnp.exp(scores - top_score), 0.0)
        denominator = lax.optimization_barrier(jnp.sum(weights, axis=2))
        rounded = lax.optimization_barrier(weights.astype(jnp.bfloat16)).astype(jnp.float32)
        context = jnp.einsum('hqk,khd->hqd', rounded, block_v, precision=lax.Precision.HIGHEST) / denominator[:, :, None]
        return context.transpose(1, 0, 2).reshape(span, INNER).astype(jnp.bfloat16)
    context = lax.map(attend_block, jnp.arange(N_ROW, dtype=jnp.int32)).reshape(TOKENS, INNER)
    residual_mid = (tokens.astype(jnp.float32) + jnp.dot(context, w_out, preferred_element_type=jnp.float32)).astype(jnp.bfloat16)
    normed_two = rms_normed(residual_mid, gain_ffn)
    gate_part = jnp.dot(normed_two, w_in[0], preferred_element_type=jnp.float32)
    up_part = jnp.dot(normed_two, w_in[1], preferred_element_type=jnp.float32)
    hidden = (jax.nn.gelu(gate_part, approximate=True) * up_part).astype(jnp.bfloat16)
    output = (residual_mid.astype(jnp.float32) + jnp.dot(hidden, w_down, preferred_element_type=jnp.float32)).astype(jnp.bfloat16)
    stacked = jnp.stack([key_rows, value_rows]).reshape(2, N_ROW, BLK_DEV, BLOCK, INNER)
    row_numbers = jnp.arange(N_ROW, dtype=jnp.int32)[:, None]
    kv_cache = jnp.zeros_like(stacked).at[:, row_numbers, slot_index].set(stacked).reshape(2, TOKENS, INNER)
    return (output, kv_cache)
```

```python
import functools

import jax
import jax.numpy as jnp
from jax import lax
from jax.experimental import pallas as pl
from jax.experimental.pallas import tpu as pltpu
from jax.sharding import PartitionSpec as P

BLOCK = 128


epsilon = 1e-06
masked_score = -1e30
VMEM = pl.BlockSpec(memory_space=pltpu.VMEM)
SMEM = pl.BlockSpec(memory_space=pltpu.SMEM)


def bias_kernel(row_ref, seg_ref, table_ref, rel_ref, out_ref):
    heads, count, width = out_ref.shape
    rows = seg_ref.shape[0]
    row = row_ref[0]
    table = table_ref[...]
    rel = rel_ref[...]
    by_distance = jnp.zeros((heads, table.shape[1]), jnp.float32)
    for bucket in range(rel.shape[1]):
        by_distance = jnp.where(table == bucket, rel[:, bucket : bucket + 1], by_distance)
    by_distance = jnp.concatenate(
        [by_distance, jnp.zeros((heads, width - table.shape[1]), jnp.float32)], axis=1
    )

    def segment_row(index):
        clipped = jnp.clip(index, 0, rows - 1)
        found = seg_ref[pl.ds(clipped, 1), :].astype(jnp.float32)
        return jnp.where(index == clipped, found, -1.0)

    own = segment_row(row)
    query_seg = jnp.broadcast_to(own, (count, count)).T
    allowed = jnp.concatenate(
        [query_seg == segment_row(row - 1), query_seg == own, query_seg == segment_row(row + 1)],
        axis=1,
    )
    for head in range(heads):
        line = jnp.broadcast_to(by_distance[head : head + 1, :], (count, width))
        shifted = pltpu.roll(line, 1, 1, stride=1, stride_axis=0)
        out_ref[head] = jnp.where(allowed, shifted, masked_score)


def masked_bias(row, segment_ids, bucket_table, rel_bias, count):
    heads = rel_bias.shape[1]
    table = jnp.pad(bucket_table, (0, 1)).reshape(1, 2 * count)
    return pl.pallas_call(
        bias_kernel,
        out_shape=jax.ShapeDtypeStruct((heads, count, 3 * count), jnp.float32),
        in_specs=[SMEM, VMEM, VMEM, VMEM],
        out_specs=VMEM,
        name="masked_bias",
    )(row.reshape(1), segment_ids.reshape(-1, count), table, rel_bias.T)


def attention_kernel(q_ref, low_ref, own_ref, high_ref, bias_ref, out_ref):
    heads, count, _ = bias_ref.shape
    width = q_ref.shape[1] // heads
    contract = (((1,), (1,)), ((), ()))
    for pair in range(0, heads, 2):
        parts = []
        for head in (pair, pair + 1):
            cut = slice(head * width, (head + 1) * width)
            query = q_ref[:, cut]
            scores = jnp.concatenate(
                [
                    lax.dot_general(
                        query, ref[0, :, cut], contract, preferred_element_type=jnp.float32
                    )
                    for ref in (low_ref, own_ref, high_ref)
                ],
                axis=1,
            )
            scores = scores + bias_ref[head]
            top = jnp.max(scores, axis=1, keepdims=True)
            weights = jnp.exp(scores - top)
            denominator = jnp.sum(weights, axis=1, keepdims=True)
            rounded = weights.astype(jnp.bfloat16)
            total = sum(
                jnp.dot(
                    rounded[:, i * count : (i + 1) * count],
                    ref[1, :, cut],
                    preferred_element_type=jnp.float32,
                )
                for i, ref in enumerate((low_ref, own_ref, high_ref))
            )
            parts.append(total / denominator)
        out_ref[:, pair * width : (pair + 2) * width] = jnp.concatenate(parts, axis=1).astype(
            out_ref.dtype
        )


def attention(queries, low, own, high, bias):
    heads, count, span = bias.shape
    return pl.pallas_call(
        attention_kernel,
        out_shape=jax.ShapeDtypeStruct(queries.shape, jnp.bfloat16),
        in_specs=[VMEM] * 5,
        out_specs=VMEM,
        cost_estimate=pl.CostEstimate(
            flops=4 * queries.size * span, bytes_accessed=4 * bias.size, transcendentals=bias.size
        ),
        name="attention",
    )(queries, low, own, high, bias)


def normed_features(shard_part, gain_vector):
    gathered = lax.all_gather(shard_part, "col", axis=1, tiled=True)
    widened = gathered.astype(jnp.float32)
    factor = lax.rsqrt(jnp.mean(widened * widened, axis=1, keepdims=True) + epsilon)
    return (widened * factor * gain_vector).astype(jnp.bfloat16)


def project_rows(normed, stacked):
    return jnp.einsum(
        "td,kdc->ktc",
        normed,
        lax.all_gather(stacked, "row", axis=1, tiled=True),
        preferred_element_type=jnp.float32,
    )


def project_columns(hidden, weight):
    partial_terms = jnp.dot(
        hidden,
        lax.all_gather(weight, "row", axis=1, tiled=True),
        preferred_element_type=jnp.float32,
    )
    return lax.psum_scatter(partial_terms, "col", scatter_dimension=1, tiled=True)


def per_device(
    tokens,
    segment_ids,
    bucket_table,
    slot_index,
    gain_attn,
    w_qkv,
    rel_bias,
    w_out,
    gain_ffn,
    w_in,
    w_down,
):
    row_count = tokens.shape[0]
    normed = normed_features(tokens, gain_attn)
    projected = project_rows(normed, w_qkv).astype(jnp.bfloat16)
    row = lax.axis_index("row")
    bias = masked_bias(row, segment_ids, bucket_table, rel_bias, row_count)
    count = lax.axis_size("row")
    forward = [(i, i + 1) for i in range(count - 1)]
    backward = [(target, source) for source, target in forward]
    low = lax.ppermute(projected[1:], "row", forward)
    high = lax.ppermute(projected[1:], "row", backward)
    context = attention(projected[0], low, projected[1:], high, bias)
    attended = project_columns(context, w_out)
    residual_mid = (tokens.astype(jnp.float32) + attended).astype(jnp.bfloat16)
    normed_two = normed_features(residual_mid, gain_ffn)
    branches = project_rows(normed_two, w_in)
    hidden = (jax.nn.gelu(branches[0], approximate=True) * branches[1]).astype(jnp.bfloat16)
    output = (residual_mid.astype(jnp.float32) + project_columns(hidden, w_down)).astype(
        jnp.bfloat16
    )
    blocks = projected[1:].reshape(2, slot_index.shape[1], BLOCK, projected.shape[2])
    kv_cache = (
        jnp.zeros_like(blocks)
        .at[:, slot_index[0]]
        .set(blocks)
        .reshape(2, row_count, projected.shape[2])
    )
    return (output, kv_cache)


def solution(mesh):
    return jax.shard_map(
        per_device,
        mesh=mesh,
        in_specs=(
            P("row", "col"),
            P(),
            P(),
            P("row", None),
            P(),
            P(None, "row", "col"),
            P(None, "col"),
            P("col", "row"),
            P(),
            P(None, "row", "col"),
            P("col", "row"),
        ),
        out_specs=(P("row", "col"), P(None, "row", "col")),
        check_vma=False,
    )
```

```python
import functools

import jax
import jax.numpy as jnp
from jax import lax
from jax.experimental import pallas as pl
from jax.experimental.pallas import tpu as pltpu
from jax.sharding import PartitionSpec as P

BLOCK = 128


epsilon = 1e-06
masked_score = -1e30
VMEM = pl.BlockSpec(memory_space=pltpu.VMEM)
SMEM = pl.BlockSpec(memory_space=pltpu.SMEM)


def bias_kernel(row_ref, seg_ref, table_ref, rel_ref, out_ref):
    heads, count, width = out_ref.shape
    rows = seg_ref.shape[0]
    row = row_ref[0]
    table = table_ref[...]
    rel = rel_ref[...]
    by_distance = jnp.zeros((heads, table.shape[1]), jnp.float32)
    for bucket in range(rel.shape[1]):
        by_distance = jnp.where(table == bucket, rel[:, bucket : bucket + 1], by_distance)
    by_distance = jnp.concatenate(
        [by_distance, jnp.zeros((heads, width - table.shape[1]), jnp.float32)], axis=1
    )

    def segment_row(index):
        clipped = jnp.clip(index, 0, rows - 1)
        found = seg_ref[pl.ds(clipped, 1), :].astype(jnp.float32)
        return jnp.where(index == clipped, found, -1.0)

    own = segment_row(row)
    query_seg = jnp.broadcast_to(own, (count, count)).T
    allowed = jnp.concatenate(
        [query_seg == segment_row(row - 1), query_seg == own, query_seg == segment_row(row + 1)],
        axis=1,
    )
    for head in range(heads):
        line = jnp.broadcast_to(by_distance[head : head + 1, :], (count, width))
        shifted = pltpu.roll(line, 1, 1, stride=1, stride_axis=0)
        out_ref[head] = jnp.where(allowed, shifted, masked_score)


def masked_bias(row, segment_ids, bucket_table, rel_bias, count):
    heads = rel_bias.shape[1]
    table = jnp.pad(bucket_table, (0, 1)).reshape(1, 2 * count)
    return pl.pallas_call(
        bias_kernel,
        out_shape=jax.ShapeDtypeStruct((heads, count, 3 * count), jnp.float32),
        in_specs=[SMEM, VMEM, VMEM, VMEM],
        out_specs=VMEM,
        name="masked_bias",
    )(row.reshape(1), segment_ids.reshape(-1, count), table, rel_bias.T)


def attention_kernel(q_ref, low_ref, own_ref, high_ref, bias_ref, out_ref):
    heads, count, _ = bias_ref.shape
    width = q_ref.shape[1] // heads
    contract = (((1,), (1,)), ((), ()))
    for pair in range(0, heads, 2):
        parts = []
        for head in (pair, pair + 1):
            cut = slice(head * width, (head + 1) * width)
            query = q_ref[:, cut]
            scores = jnp.concatenate(
                [
                    lax.dot_general(
                        query, ref[0, :, cut], contract, preferred_element_type=jnp.float32
                    )
                    for ref in (low_ref, own_ref, high_ref)
                ],
                axis=1,
            )
            scores = scores + bias_ref[head]
            top = jnp.max(scores, axis=1, keepdims=True)
            weights = jnp.exp(scores - top)
            denominator = jnp.sum(weights, axis=1, keepdims=True)
            rounded = weights.astype(jnp.bfloat16)
            total = sum(
                jnp.dot(
                    rounded[:, i * count : (i + 1) * count],
                    ref[1, :, cut],
                    preferred_element_type=jnp.float32,
                )
                for i, ref in enumerate((low_ref, own_ref, high_ref))
            )
            parts.append(total / denominator)
        out_ref[:, pair * width : (pair + 2) * width] = jnp.concatenate(parts, axis=1).astype(
            out_ref.dtype
        )


def attention(queries, low, own, high, bias):
    heads, count, span = bias.shape
    return pl.pallas_call(
        attention_kernel,
        out_shape=jax.ShapeDtypeStruct(queries.shape, jnp.bfloat16),
        in_specs=[VMEM] * 5,
        out_specs=VMEM,
        cost_estimate=pl.CostEstimate(
            flops=4 * queries.size * span, bytes_accessed=4 * bias.size, transcendentals=bias.size
        ),
        name="attention",
    )(queries, low, own, high, bias)


def exchange(value, axis, partner):
    count = lax.axis_size(axis)
    return lax.ppermute(value, axis, [(i, partner(i) % count) for i in range(count)])


def other_core(value):
    return exchange(value, "row", lambda i: i ^ 1)


def pair_exchange(value, step):
    return exchange(value, "row", lambda i: i ^ (2 * step))


def shifted(value, step):
    return exchange(value, "col", lambda i: i + step)


def after(value, *earlier):
    return lax.optimization_barrier((value, *earlier))[0]


def near_pieces(weight):
    pairs = lax.axis_size("row") // 2
    if pairs == 4:
        return [pair_exchange(weight, 1), pair_exchange(weight, 2)]
    return [pair_exchange(weight, step) for step in range(1, pairs)]


def far_pieces(near, axis):
    if len(near) != 2:
        return []
    first, _ = jnp.split(near[0], 2, axis=axis)
    _, second = jnp.split(near[1], 2, axis=axis)
    return [pair_exchange(first, 2), pair_exchange(second, 1)]


def project_kernel(split, place_ref, scale_ref, gain_ref, *refs):
    blocks = lax.axis_size("col")
    token_refs, refs = refs[:blocks], refs[blocks:]
    *weight_refs, own_ref, send_ref, held = refs
    row, col = place_ref[0], place_ref[1]
    pair, core = row // 2, row % 2
    scale = scale_ref[...]
    for step in range(blocks):
        block = lax.rem(col - step + blocks, blocks)
        gain = gain_ref[pl.ds(2 * block + core, 1), :]
        held[block] = (token_refs[step][...].astype(jnp.float32) * scale * gain).astype(
            jnp.bfloat16
        )
    far = len(weight_refs) == blocks + 1
    direct = blocks - 1 if far else blocks
    count = own_ref.shape[0]
    parts, width = weight_refs[0].shape[0], weight_refs[0].shape[2]
    tile = min(256, width)
    for part in range(parts):
        for start in range(0, width, tile):
            stop = min(start + tile, width)
            total = None
            for step in range(blocks):
                if step < direct:
                    weight = weight_refs[step][part, :, start:stop]
                elif split == 0:
                    weight = weight_refs[direct + part][0, :, start:stop]
                else:
                    half = start // (width // 2)
                    offset = start - half * (width // 2)
                    weight = weight_refs[direct + half][part, :, offset : offset + stop - start]
                term = jnp.dot(held[pair ^ step], weight, preferred_element_type=jnp.float32)
                total = term if total is None else total + term
            place = slice(part * width + start, part * width + stop)
            own_ref[:, place] = total[:count]
            send_ref[:, place] = total[count:].astype(send_ref.dtype)


def project(place, scale, gain, token_blocks, pieces, split, name):
    tokens_two, depth = token_blocks[0].shape
    columns = pieces[0].shape[0] * pieces[0].shape[2]
    count = tokens_two // 2
    return pl.pallas_call(
        functools.partial(project_kernel, split),
        out_shape=(
            jax.ShapeDtypeStruct((count, columns), jnp.float32),
            jax.ShapeDtypeStruct((count, columns), jnp.bfloat16),
        ),
        in_specs=[SMEM] + [VMEM] * (2 + len(token_blocks) + len(pieces)),
        out_specs=(VMEM, VMEM),
        scratch_shapes=[pltpu.VMEM((len(token_blocks), tokens_two, depth), jnp.bfloat16)],
        compiler_params=pltpu.CompilerParams(vmem_limit_bytes=40 << 20),
        cost_estimate=pl.CostEstimate(
            flops=2 * tokens_two * depth * len(token_blocks) * columns,
            bytes_accessed=2 * depth * len(token_blocks) * columns,
            transcendentals=0,
        ),
        name=name,
    )(place, scale, gain, *token_blocks, *pieces)


def columns_kernel(place_ref, own_in_ref, other_in_ref, *refs):
    blocks = lax.axis_size("col")
    *weight_refs, own_ref = refs[: len(refs) - blocks]
    send_refs, held = refs[len(refs) - blocks : -1], refs[-1]
    row, col = place_ref[0], place_ref[1]
    pair = row // 2
    hidden = jnp.concatenate([own_in_ref[...], other_in_ref[...]], axis=0)
    far = len(weight_refs) == blocks + 1
    direct = blocks - 1 if far else blocks
    for step in range(blocks):
        if step < direct:
            total = jnp.dot(hidden, weight_refs[step][...], preferred_element_type=jnp.float32)
        else:
            half = hidden.shape[1] // 2
            total = jnp.dot(
                hidden[:, :half], weight_refs[direct][...], preferred_element_type=jnp.float32
            ) + jnp.dot(
                hidden[:, half:], weight_refs[direct + 1][...], preferred_element_type=jnp.float32
            )
        held[lax.rem((pair ^ step) - col + blocks, blocks)] = total
    own_ref[...] = held[0]
    for step in range(1, blocks):
        send_refs[step - 1][...] = held[step].astype(jnp.bfloat16)


def columns(place, own, other, pieces, name):
    count, depth = own.shape
    width = pieces[0].shape[1]
    blocks = lax.axis_size("col")
    return pl.pallas_call(
        columns_kernel,
        out_shape=(
            jax.ShapeDtypeStruct((2 * count, width), jnp.float32),
            *[jax.ShapeDtypeStruct((2 * count, width), jnp.bfloat16)] * (blocks - 1),
        ),
        in_specs=[SMEM] + [VMEM] * (2 + len(pieces)),
        out_specs=tuple([VMEM] * blocks),
        scratch_shapes=[pltpu.VMEM((blocks, 2 * count, width), jnp.float32)],
        compiler_params=pltpu.CompilerParams(vmem_limit_bytes=40 << 20),
        cost_estimate=pl.CostEstimate(
            flops=4 * count * depth * width * blocks,
            bytes_accessed=2 * depth * width * blocks,
            transcendentals=0,
        ),
        name=name,
    )(place, own, other, *pieces)


def summed(own, sends, residual):
    total = own + residual.astype(jnp.float32)
    for step, send in enumerate(sends, 1):
        total = total + shifted(send, step).astype(jnp.float32)
    return total.astype(jnp.bfloat16)


def gathered(block):
    return [block] + [shifted(block, step) for step in range(1, lax.axis_size("col"))]


def square_sums(blocks):
    return sum(jnp.sum(jnp.square(b.astype(jnp.float32)), axis=1) for b in blocks)


def per_device(
    tokens,
    segment_ids,
    bucket_table,
    slot_index,
    gain_attn,
    w_qkv,
    rel_bias,
    w_out,
    gain_ffn,
    w_in,
    w_down,
):
    rows, cols = lax.axis_size("row"), lax.axis_size("col")
    count, width = tokens.shape
    half = width // 2
    features = width * cols
    row, col = lax.axis_index("row"), lax.axis_index("col")
    core = row % 2
    place = jnp.stack([row, col]).astype(jnp.int32)

    qkv_near = near_pieces(w_qkv)

    kept = jnp.where(core == 0, tokens[:, :half], tokens[:, half:])
    given = jnp.where(core == 0, tokens[:, half:], tokens[:, :half])
    token_block = jnp.concatenate([kept, other_core(given)], axis=0)
    token_blocks = gathered(token_block)
    squares = square_sums(token_blocks)
    squares = squares + jnp.roll(other_core(squares), count)
    scale = lax.rsqrt(squares / features + epsilon)[:, None]
    bias = masked_bias(row, segment_ids, bucket_table, rel_bias, count)

    out_near = near_pieces(after(w_out, *qkv_near))
    qkv_far = far_pieces(qkv_near, 2)
    in_near = near_pieces(after(w_in, *(qkv_far or qkv_near)))
    own, send = project(
        place, scale, gain_attn.reshape(rows, -1), token_blocks, [w_qkv, *qkv_near, *qkv_far], 2, "qkv"
    )
    projected = (own + other_core(send).astype(jnp.float32)).astype(jnp.bfloat16)
    projected = projected.reshape(count, 3, width).transpose(1, 0, 2)
    forward = [(i, i + 1) for i in range(rows - 1)]
    backward = [(target, source) for source, target in forward]
    low = lax.ppermute(projected[1:], "row", forward)
    high = lax.ppermute(projected[1:], "row", backward)
    out_far = far_pieces(out_near, 0)
    context = attention(projected[0], low, projected[1:], high, bias)
    own, *sends = columns(
        place, context, other_core(context), [w_out, *out_near, *out_far], "attention_out"
    )
    middle = summed(own, sends, token_block)

    middle_blocks = gathered(middle)
    squares = square_sums(middle_blocks)
    squares = squares[:count] + other_core(squares[count:])
    scale = lax.rsqrt(squares / features + epsilon)[:, None]
    in_far = far_pieces(in_near, 0)
    down_near = near_pieces(after(w_down, *in_near))
    down_far = far_pieces(down_near, 0)
    own, send = project(
        place,
        jnp.ones((2 * count, 1), jnp.float32),
        gain_ffn.reshape(rows, -1),
        middle_blocks,
        [w_in, *in_near, *in_far],
        0,
        "ffn_in",
    )
    branches = (own + other_core(send).astype(jnp.float32)) * scale
    inner = branches.shape[1] // 2
    hidden = (
        jax.nn.gelu(branches[:, :inner], approximate=True) * branches[:, inner:]
    ).astype(jnp.bfloat16)
    own, *sends = columns(
        place, hidden, other_core(hidden), [w_down, *down_near, *down_far], "ffn_out"
    )
    result = summed(own, sends, middle)
    received = other_core(result[count:])
    output = jnp.where(
        core == 0,
        jnp.concatenate([result[:count], received], axis=1),
        jnp.concatenate([received, result[:count]], axis=1),
    )

    blocks = projected[1:].reshape(2, slot_index.shape[1], BLOCK, width)
    kv_cache = (
        jnp.zeros_like(blocks).at[:, slot_index[0]].set(blocks).reshape(2, count, width)
    )
    return (output, kv_cache)


def solution(mesh):
    return jax.shard_map(
        per_device,
        mesh=mesh,
        in_specs=(
            P("row", "col"),
            P(),
            P(),
            P("row", None),
            P(),
            P(None, "row", "col"),
            P(None, "col"),
            P("col", "row"),
            P(),
            P(None, "row", "col"),
            P("col", "row"),
        ),
        out_specs=(P("row", "col"), P(None, "row", "col")),
        check_vma=False,
    )
```

```python
import functools

import jax
import jax.numpy as jnp
from jax import lax
from jax.experimental import pallas as pl
from jax.experimental.pallas import tpu as pltpu
from jax.sharding import PartitionSpec as P

BLOCK = 128


epsilon = 1e-06
masked_score = -1e30
VMEM = pl.BlockSpec(memory_space=pltpu.VMEM)
SMEM = pl.BlockSpec(memory_space=pltpu.SMEM)


def bias_kernel(row_ref, seg_ref, table_ref, rel_ref, out_ref):
    heads, count, width = out_ref.shape
    rows = seg_ref.shape[0]
    row = row_ref[0]
    table = table_ref[...]
    rel = rel_ref[...]
    by_distance = jnp.zeros((heads, table.shape[1]), jnp.float32)
    for bucket in range(rel.shape[1]):
        by_distance = jnp.where(table == bucket, rel[:, bucket : bucket + 1], by_distance)
    by_distance = jnp.concatenate(
        [by_distance, jnp.zeros((heads, width - table.shape[1]), jnp.float32)], axis=1
    )

    def segment_row(index):
        clipped = jnp.clip(index, 0, rows - 1)
        found = seg_ref[pl.ds(clipped, 1), :].astype(jnp.float32)
        return jnp.where(index == clipped, found, -1.0)

    own = segment_row(row)
    query_seg = jnp.broadcast_to(own, (count, count)).T
    allowed = jnp.concatenate(
        [query_seg == segment_row(row - 1), query_seg == own, query_seg == segment_row(row + 1)],
        axis=1,
    )
    for head in range(heads):
        line = jnp.broadcast_to(by_distance[head : head + 1, :], (count, width))
        shifted = pltpu.roll(line, 1, 1, stride=1, stride_axis=0)
        out_ref[head] = jnp.where(allowed, shifted, masked_score)


def masked_bias(row, segment_ids, bucket_table, rel_bias, count):
    heads = rel_bias.shape[1]
    table = jnp.pad(bucket_table, (0, 1)).reshape(1, 2 * count)
    return pl.pallas_call(
        bias_kernel,
        out_shape=jax.ShapeDtypeStruct((heads, count, 3 * count), jnp.float32),
        in_specs=[SMEM, VMEM, VMEM, VMEM],
        out_specs=VMEM,
        name="masked_bias",
    )(row.reshape(1), segment_ids.reshape(-1, count), table, rel_bias.T)


def attention_kernel(q_ref, *refs):
    *key_refs, bias_ref, out_ref = refs
    key_refs, value_refs = key_refs[:3], key_refs[3:]
    heads, count, _ = bias_ref.shape
    width = q_ref.shape[1] // heads
    contract = (((1,), (1,)), ((), ()))
    parts = []
    for head in range(heads):
        cut = slice(head * width, (head + 1) * width)
        query = q_ref[:, cut]
        scores = jnp.concatenate(
            [
                lax.dot_general(query, ref[:, cut], contract, preferred_element_type=jnp.float32)
                for ref in key_refs
            ],
            axis=1,
        )
        scores = scores + bias_ref[head]
        top = jnp.max(scores, axis=1, keepdims=True)
        weights = jnp.exp(scores - top)
        denominator = jnp.sum(weights, axis=1, keepdims=True)
        rounded = weights.astype(jnp.bfloat16)
        total = sum(
            jnp.dot(
                rounded[:, i * count : (i + 1) * count],
                ref[:, cut],
                preferred_element_type=jnp.float32,
            )
            for i, ref in enumerate(value_refs)
        )
        parts.append(total / denominator)
    out_ref[...] = jnp.concatenate(parts, axis=1).astype(out_ref.dtype)


def attention(queries, low, own, high, bias):
    heads, count, span = bias.shape
    width = queries.shape[1]
    steps = heads // 2
    lanes = width // steps
    keys = pl.BlockSpec((count, lanes), lambda i: (0, i))
    values = pl.BlockSpec((count, lanes), lambda i: (0, i + steps))
    return pl.pallas_call(
        attention_kernel,
        out_shape=jax.ShapeDtypeStruct((count, width), jnp.bfloat16),
        grid=(steps,),
        in_specs=[keys] * 4 + [values] * 3 + [pl.BlockSpec((2, count, span), lambda i: (i, 0, 0))],
        out_specs=keys,
        cost_estimate=pl.CostEstimate(
            flops=4 * queries.size * span, bytes_accessed=4 * bias.size, transcendentals=bias.size
        ),
        name="attention",
    )(queries, low, own, high, low, own, high, bias)


def exchange(value, axis, partner):
    count = lax.axis_size(axis)
    return lax.ppermute(value, axis, [(i, partner(i) % count) for i in range(count)])


def other_core(value):
    return exchange(value, "row", lambda i: i ^ 1)


def pair_exchange(value, step):
    return exchange(value, "row", lambda i: i ^ (2 * step))


def shifted(value, step):
    return exchange(value, "col", lambda i: i + step)


def after(value, *earlier):
    return lax.optimization_barrier((value, *earlier))[0]


def near_pieces(weight):
    pairs = lax.axis_size("row") // 2
    if pairs == 4:
        return [pair_exchange(weight, 1), pair_exchange(weight, 2)]
    return [pair_exchange(weight, step) for step in range(1, pairs)]


def after_all(values, *earlier):
    return list(lax.optimization_barrier((*values, *earlier))[: len(values)])


def first_hop(weight, *earlier):
    weight = after(weight, *earlier)
    return weight, near_pieces(weight)


def far_pieces(near, axis):
    if len(near) != 2:
        return []
    first, _ = jnp.split(near[0], 2, axis=axis)
    _, second = jnp.split(near[1], 2, axis=axis)
    return [pair_exchange(first, 2), pair_exchange(second, 1)]


def norm_kernel(place_ref, gain_ref, *refs):
    *block_refs, kept_ref, given_ref = refs
    blocks = len(block_refs)
    core, col = lax.rem(place_ref[0], 2), place_ref[1]
    wide = [ref[...].astype(jnp.float32) for ref in block_refs]
    squares = sum(jnp.sum(block * block, axis=1, keepdims=True) for block in wide)
    half = wide[0].shape[1] // 2
    scale = lax.rsqrt(squares / (2 * half * blocks) + epsilon)
    for step, block in enumerate(wide):
        index = lax.rem(col - step + blocks, blocks)
        normed = (block * scale * gain_ref[pl.ds(index, 1), :]).astype(jnp.bfloat16)
        low, high = normed[:, :half], normed[:, half:]
        kept_ref[index] = jnp.where(core == 0, low, high)
        given_ref[index] = jnp.where(core == 0, high, low)


def norm_tokens(place, gain, token_blocks):
    count, width = token_blocks[0].shape
    shape = jax.ShapeDtypeStruct((len(token_blocks), count, width // 2), jnp.bfloat16)
    return pl.pallas_call(
        norm_kernel,
        out_shape=(shape, shape),
        in_specs=[SMEM] + [VMEM] * (1 + len(token_blocks)),
        out_specs=(VMEM, VMEM),
        name="norm_tokens",
    )(place, gain, *token_blocks)


def multiply_pieces(groups, held, pair, piece, width, own_refs, send_refs):
    blocks, tokens_two, _ = held.shape
    count = tokens_two // 2
    tile = min(256, width, held.shape[2])
    for group, own_ref, send_ref in zip(groups, own_refs, send_refs):
        for place, part in enumerate(group):
            for start in range(0, width, tile):
                stop = min(start + tile, width)
                total = None
                for step in range(blocks):
                    weight = piece(step, part, start, stop)
                    term = jnp.dot(held[pair ^ step], weight, preferred_element_type=jnp.float32)
                    total = term if total is None else total + term
                where = slice(place * width + start, place * width + stop)
                own_ref[:, where] = total[:count]
                send_ref[:, where] = total[count:].astype(send_ref.dtype)


def pack_kernel(qkv_ref, out_ref, packed_ref):
    parts, depth, width = qkv_ref.shape
    row = 0
    for part in range(parts):
        for start in range(0, width, depth):
            packed_ref[row : row + depth, :] = qkv_ref[part, :, start : start + depth]
            row += depth
    packed_ref[row:, :] = out_ref[...]


def packed(w_qkv, w_out):
    parts, depth, width = w_qkv.shape
    count = parts * width // depth
    return pl.pallas_call(
        pack_kernel,
        out_shape=jax.ShapeDtypeStruct((count * depth + width, depth), w_qkv.dtype),
        in_specs=[VMEM, VMEM],
        out_specs=VMEM,
        name="pack",
    )(w_qkv, w_out)


def qkv_kernel(place_ref, own_in_ref, other_in_ref, *refs):
    *weight_refs, own_q, own_kv, send_q, send_kv, held = refs
    count = own_in_ref.shape[1]
    held[:, :count] = own_in_ref[...]
    held[:, count:] = other_in_ref[...]
    blocks, depth = held.shape[0], weight_refs[0].shape[1]
    direct = blocks - 1 if len(weight_refs) == blocks + 1 else blocks
    width = own_q.shape[1]

    def piece(step, part, start, stop):
        row = (part * width // depth + start // depth) * depth
        offset = start % depth
        if step < direct:
            return weight_refs[step][row : row + depth, offset : offset + stop - start]
        half = weight_refs[direct].shape[0]
        row = row - row // half * half
        which = (part * width + start) // (half // depth * depth)
        return weight_refs[direct + which][row : row + depth, offset : offset + stop - start]

    multiply_pieces(
        ((0,), (1, 2)), held, place_ref[0] // 2, piece, width, (own_q, own_kv), (send_q, send_kv)
    )


def project_qkv(place, own, other, pieces):
    blocks, count, depth = own.shape
    width = 2 * depth
    shapes = [jax.ShapeDtypeStruct((count, n * width), jnp.float32) for n in (1, 2)] * 2
    return pl.pallas_call(
        qkv_kernel,
        out_shape=tuple(shapes),
        in_specs=[SMEM] + [VMEM] * (2 + len(pieces)),
        out_specs=tuple([VMEM] * 4),
        scratch_shapes=[pltpu.VMEM((blocks, 2 * count, depth), jnp.bfloat16)],
        compiler_params=pltpu.CompilerParams(vmem_limit_bytes=16 << 20),
        cost_estimate=pl.CostEstimate(
            flops=12 * count * depth * blocks * width,
            bytes_accessed=6 * depth * blocks * width,
            transcendentals=0,
        ),
        name="qkv",
    )(place, own, other, *pieces)


def ffn_in_kernel(place_ref, gain_ref, *refs):
    blocks = lax.axis_size("col")
    block_refs, refs = refs[:blocks], refs[blocks:]
    *weight_refs, own_ref, send_ref, held = refs
    row, col = place_ref[0], place_ref[1]
    for step, ref in enumerate(block_refs):
        index = lax.rem(col - step + blocks, blocks)
        gain = gain_ref[pl.ds(2 * index + lax.rem(row, 2), 1), :]
        held[index] = (ref[...].astype(jnp.float32) * gain).astype(jnp.bfloat16)
    direct = blocks - 1 if len(weight_refs) == blocks + 1 else blocks

    def piece(step, part, start, stop):
        if step < direct:
            return weight_refs[step][part, :, start:stop]
        return weight_refs[direct + part][0, :, start:stop]

    width = weight_refs[0].shape[2]
    multiply_pieces(((0, 1),), held, row // 2, piece, width, (own_ref,), (send_ref,))


def project_ffn(place, gain, token_blocks, pieces):
    tokens_two, depth = token_blocks[0].shape
    blocks, count = len(token_blocks), tokens_two // 2
    columns = 2 * pieces[0].shape[2]
    return pl.pallas_call(
        ffn_in_kernel,
        out_shape=(
            jax.ShapeDtypeStruct((count, columns), jnp.float32),
            jax.ShapeDtypeStruct((count, columns), jnp.bfloat16),
        ),
        in_specs=[SMEM] + [VMEM] * (1 + blocks + len(pieces)),
        out_specs=(VMEM, VMEM),
        scratch_shapes=[pltpu.VMEM((blocks, tokens_two, depth), jnp.bfloat16)],
        compiler_params=pltpu.CompilerParams(vmem_limit_bytes=16 << 20),
        cost_estimate=pl.CostEstimate(
            flops=2 * tokens_two * depth * blocks * columns,
            bytes_accessed=2 * depth * blocks * columns,
            transcendentals=0,
        ),
        name="ffn_in",
    )(place, gain, *token_blocks, *pieces)


def columns_kernel(first, place_ref, own_in_ref, other_in_ref, *refs):
    blocks = lax.axis_size("col")
    *weight_refs, own_ref = refs[: len(refs) - blocks]
    send_refs, held = refs[len(refs) - blocks : -1], refs[-1]
    row, col = place_ref[0], place_ref[1]
    pair = row // 2
    hidden = jnp.concatenate([own_in_ref[...], other_in_ref[...]], axis=0)
    far = len(weight_refs) == blocks + 1
    direct = blocks - 1 if far else blocks
    for step in range(blocks):
        if step < direct:
            total = jnp.dot(hidden, weight_refs[step][first:, :], preferred_element_type=jnp.float32)
        elif first:
            skipped = first - weight_refs[direct].shape[0]
            total = jnp.dot(
                hidden, weight_refs[direct + 1][skipped:, :], preferred_element_type=jnp.float32
            )
        else:
            half = hidden.shape[1] // 2
            total = jnp.dot(
                hidden[:, :half], weight_refs[direct][...], preferred_element_type=jnp.float32
            ) + jnp.dot(
                hidden[:, half:], weight_refs[direct + 1][...], preferred_element_type=jnp.float32
            )
        held[lax.rem((pair ^ step) - col + blocks, blocks)] = total
    own_ref[...] = held[0]
    for step in range(1, blocks):
        send_refs[step - 1][...] = held[step].astype(jnp.bfloat16)


def columns(place, own, other, pieces, name):
    count, depth = own.shape
    width = pieces[0].shape[1]
    blocks = lax.axis_size("col")
    return pl.pallas_call(
        functools.partial(columns_kernel, pieces[0].shape[0] - depth),
        out_shape=(
            jax.ShapeDtypeStruct((2 * count, width), jnp.float32),
            *[jax.ShapeDtypeStruct((2 * count, width), jnp.bfloat16)] * (blocks - 1),
        ),
        in_specs=[SMEM] + [VMEM] * (2 + len(pieces)),
        out_specs=tuple([VMEM] * blocks),
        scratch_shapes=[pltpu.VMEM((blocks, 2 * count, width), jnp.float32)],
        compiler_params=pltpu.CompilerParams(vmem_limit_bytes=16 << 20),
        cost_estimate=pl.CostEstimate(
            flops=4 * count * depth * width * blocks,
            bytes_accessed=2 * depth * width * blocks,
            transcendentals=0,
        ),
        name=name,
    )(place, own, other, *pieces)


def summed(own, sends, residual):
    total = own + residual.astype(jnp.float32)
    for step, send in enumerate(sends, 1):
        total = total + shifted(send, step).astype(jnp.float32)
    return total.astype(jnp.bfloat16)


def gathered(block):
    return [block] + [shifted(block, step) for step in range(1, lax.axis_size("col"))]


def square_sums(blocks):
    return sum(jnp.sum(jnp.square(b.astype(jnp.float32)), axis=1) for b in blocks)


def per_device(
    tokens,
    segment_ids,
    bucket_table,
    slot_index,
    gain_attn,
    w_qkv,
    rel_bias,
    w_out,
    gain_ffn,
    w_in,
    w_down,
):
    rows, cols = lax.axis_size("row"), lax.axis_size("col")
    count, width = tokens.shape
    half = width // 2
    features = width * cols
    row, col = lax.axis_index("row"), lax.axis_index("col")
    core = row % 2
    place = jnp.stack([row, col]).astype(jnp.int32)

    first = packed(w_qkv, w_out)
    first_near = near_pieces(first)
    token_blocks = gathered(tokens)
    kept, given = norm_tokens(place, gain_attn.reshape(cols, width), token_blocks)
    received = other_core(after(given, *first_near))
    token_block = jnp.concatenate(
        [
            jnp.where(core == 0, tokens[:, :half], tokens[:, half:]),
            other_core(jnp.where(core == 0, tokens[:, half:], tokens[:, :half])),
        ],
        axis=0,
    )
    bias = masked_bias(row, segment_ids, bucket_table, rel_bias, count)
    first_far = far_pieces(first_near, 0)
    first_pieces = [first, *first_near, *first_far]
    w_down, down_near = first_hop(w_down, received)
    kept, bias, token_block = lax.optimization_barrier((kept, bias, token_block))
    own_q, own_kv, send_q, send_kv = project_qkv(
        place, kept, received, first_pieces
    )
    key_value = (own_kv + other_core(send_kv)).astype(jnp.bfloat16)
    queries = (own_q + other_core(after(send_q, key_value))).astype(jnp.bfloat16)
    forward = [(i, i + 1) for i in range(rows - 1)]
    backward = [(target, source) for source, target in forward]
    low = lax.ppermute(key_value, "row", forward)
    high = lax.ppermute(key_value, "row", backward)
    low, high, *down_near = lax.optimization_barrier((low, high, *down_near))
    in_near = near_pieces(after(w_in, low, high, *down_near))
    context = attention(queries, low, key_value, high, bias)
    own, *sends = columns(
        place, context, other_core(context), first_pieces, "attention_out"
    )
    middle = summed(own, sends, token_block)
    in_far = far_pieces(after_all(in_near, middle), 0)

    middle_blocks = gathered(middle)
    squares = square_sums(middle_blocks)
    squares = squares[:count] + other_core(squares[count:])
    scale = lax.rsqrt(squares / features + epsilon)[:, None]
    down_far = far_pieces(after_all(down_near, middle_blocks[1]), 0)
    own, send = project_ffn(
        place, gain_ffn.reshape(rows, -1), middle_blocks, [w_in, *in_near, *in_far]
    )
    other_sum, *down_far = lax.optimization_barrier((other_core(send), *down_far))
    branches = (own + other_sum.astype(jnp.float32)) * scale
    inner = branches.shape[1] // 2
    hidden = (
        jax.nn.gelu(branches[:, :inner], approximate=True) * branches[:, inner:]
    ).astype(jnp.bfloat16)
    own, *sends = columns(
        place, hidden, other_core(hidden), [w_down, *down_near, *down_far], "ffn_out"
    )
    result = summed(own, sends, middle)
    received = other_core(result[count:])
    output = jnp.where(
        core == 0,
        jnp.concatenate([result[:count], received], axis=1),
        jnp.concatenate([received, result[:count]], axis=1),
    )

    stacked = jnp.stack([key_value[:, :width], key_value[:, width:]])
    blocks = stacked.reshape(2, slot_index.shape[1], BLOCK, width)
    kv_cache = (
        jnp.zeros_like(blocks).at[:, slot_index[0]].set(blocks).reshape(2, count, width)
    )
    return (output, kv_cache)


def solution(mesh):
    return jax.shard_map(
        per_device,
        mesh=mesh,
        in_specs=(
            P("row", "col"),
            P(),
            P(),
            P("row", None),
            P(),
            P(None, "row", "col"),
            P(None, "col"),
            P("col", "row"),
            P(),
            P(None, "row", "col"),
            P("col", "row"),
        ),
        out_specs=(P("row", "col"), P(None, "row", "col")),
        check_vma=False,
    )
```

```python
import functools

import jax
import jax.numpy as jnp
from jax import lax
from jax.experimental import pallas as pl
from jax.experimental.pallas import tpu as pltpu
from jax.sharding import PartitionSpec as P

BLOCK = 128


epsilon = 1e-06
masked_score = -1e30
VMEM = pl.BlockSpec(memory_space=pltpu.VMEM)
SMEM = pl.BlockSpec(memory_space=pltpu.SMEM)


def bias_kernel(row_ref, seg_ref, table_ref, rel_ref, out_ref):
    heads, count, width = out_ref.shape
    rows = seg_ref.shape[0]
    row = row_ref[0]
    table = table_ref[...]
    rel = rel_ref[...]
    by_distance = jnp.zeros((heads, table.shape[1]), jnp.float32)
    for bucket in range(rel.shape[1]):
        by_distance = jnp.where(table == bucket, rel[:, bucket : bucket + 1], by_distance)
    by_distance = jnp.concatenate(
        [by_distance, jnp.zeros((heads, width - table.shape[1]), jnp.float32)], axis=1
    )

    def segment_row(index):
        clipped = jnp.clip(index, 0, rows - 1)
        found = seg_ref[pl.ds(clipped, 1), :].astype(jnp.float32)
        return jnp.where(index == clipped, found, -1.0)

    own = segment_row(row)
    query_seg = jnp.broadcast_to(own, (count, count)).T
    allowed = jnp.concatenate(
        [query_seg == segment_row(row - 1), query_seg == own, query_seg == segment_row(row + 1)],
        axis=1,
    )
    for head in range(heads):
        line = jnp.broadcast_to(by_distance[head : head + 1, :], (count, width))
        shifted = pltpu.roll(line, 1, 1, stride=1, stride_axis=0)
        out_ref[head] = jnp.where(allowed, shifted, masked_score)


def masked_bias(row, segment_ids, bucket_table, rel_bias, count):
    heads = rel_bias.shape[1]
    table = jnp.pad(bucket_table, (0, 1)).reshape(1, 2 * count)
    return pl.pallas_call(
        bias_kernel,
        out_shape=jax.ShapeDtypeStruct((heads, count, 3 * count), jnp.float32),
        in_specs=[SMEM, VMEM, VMEM, VMEM],
        out_specs=VMEM,
        compiler_params=pltpu.CompilerParams(vmem_limit_bytes=8 << 20),
        name="masked_bias",
    )(row.reshape(1), segment_ids.reshape(-1, count), table, rel_bias.T)


def attention_kernel(q_ref, low_ref, own_ref, high_ref, bias_ref, out_ref):
    heads, count, _ = bias_ref.shape
    total_width = q_ref.shape[1]
    width = total_width // heads
    sides = (low_ref, own_ref, high_ref)
    for pair in range(0, heads, 2):
        parts = []
        for head in (pair, pair + 1):
            cut = slice(head * width, (head + 1) * width)
            after_keys = slice(total_width + head * width, total_width + (head + 1) * width)
            query = q_ref[:, cut]
            scores = jnp.concatenate(
                [
                    lax.dot_general(
                        query,
                        ref[:, cut],
                        (((1,), (1,)), ((), ())),
                        preferred_element_type=jnp.float32,
                    )
                    for ref in sides
                ],
                axis=1,
            )
            scores = scores + bias_ref[head]
            top = jnp.max(scores, axis=1, keepdims=True)
            weights = jnp.exp(scores - top)
            denominator = jnp.sum(weights, axis=1, keepdims=True)
            rounded = weights.astype(jnp.bfloat16)
            total = sum(
                jnp.dot(
                    rounded[:, i * count : (i + 1) * count],
                    ref[:, after_keys],
                    preferred_element_type=jnp.float32,
                )
                for i, ref in enumerate(sides)
            )
            parts.append(total / denominator)
        out_ref[:, pair * width : (pair + 2) * width] = jnp.concatenate(parts, axis=1).astype(
            out_ref.dtype
        )


def attention(queries, low, own, high, bias):
    count, span = bias.shape[1:]
    return pl.pallas_call(
        attention_kernel,
        out_shape=jax.ShapeDtypeStruct(queries.shape, jnp.bfloat16),
        in_specs=[VMEM] * 5,
        out_specs=VMEM,
        compiler_params=pltpu.CompilerParams(vmem_limit_bytes=16 << 20),
        cost_estimate=pl.CostEstimate(
            flops=4 * queries.size * span, bytes_accessed=4 * bias.size, transcendentals=bias.size
        ),
        name="attention",
    )(queries, low, own, high, bias)


def exchange(value, axis, partner):
    count = lax.axis_size(axis)
    return lax.ppermute(value, axis, [(i, partner(i) % count) for i in range(count)])


def other_core(value):
    return exchange(value, "row", lambda i: i ^ 1)


def pair_exchange(value, step):
    return exchange(value, "row", lambda i: i ^ (2 * step))


def shifted(value, step):
    return exchange(value, "col", lambda i: i + step)


def after(value, *earlier):
    return lax.optimization_barrier((value, *earlier))[0]


def near_pieces(weight):
    pairs = lax.axis_size("row") // 2
    if pairs == 4:
        return [pair_exchange(weight, 1), pair_exchange(weight, 2)]
    return [pair_exchange(weight, step) for step in range(1, pairs)]


def after_all(values, *earlier):
    return list(lax.optimization_barrier((*values, *earlier))[: len(values)])


def first_hop(weight, *earlier):
    weight = after(weight, *earlier)
    return weight, near_pieces(weight)


def first_phase(low, high):
    pairs = lax.axis_size("row") // 2
    if pairs != 4:
        return [pair_exchange(part, step) for step in range(1, pairs) for part in (low, high)]
    return [pair_exchange(low, 1), pair_exchange(high, 2)]


def packet_kernel(own_ref, low_in, high_in, low_ref, high_ref):
    size = low_in.shape[0]
    low_ref[0], high_ref[0] = own_ref[0], own_ref[1]
    low_ref[1], high_ref[1] = low_in[...], high_in[...]


def second_phase(own, first):
    if len(first) != 2:
        return []
    shape = jax.ShapeDtypeStruct(own.shape, own.dtype)
    low, high = pl.pallas_call(
        packet_kernel,
        out_shape=(shape, shape),
        in_specs=[VMEM] * 3,
        out_specs=(VMEM, VMEM),
        compiler_params=pltpu.CompilerParams(vmem_limit_bytes=8 << 20),
        name="packet",
    )(own, *first)
    return [pair_exchange(high, 1), pair_exchange(low, 2)]


def half_ref(refs, step, part):
    own, *others = refs
    if step == 0:
        return own.at[part]
    if len(others) != 4:
        return others[2 * (step - 1) + part]
    near_low, side_high, highs, lows = others
    if step == 3:
        return (highs if part else lows).at[1]
    if part == step - 1:
        return near_low if part == 0 else side_high
    return (highs if part else lows).at[0]


def norm_kernel(place_ref, gain_ref, *refs):
    *block_refs, kept_ref, given_ref = refs
    blocks = len(block_refs)
    core, col = lax.rem(place_ref[0], 2), place_ref[1]
    wide = [ref[...].astype(jnp.float32) for ref in block_refs]
    squares = sum(jnp.sum(block * block, axis=1, keepdims=True) for block in wide)
    half = wide[0].shape[1] // 2
    scale = lax.rsqrt(squares / (2 * half * blocks) + epsilon)
    for step, block in enumerate(wide):
        index = lax.rem(col - step + blocks, blocks)
        normed = (block * scale * gain_ref[pl.ds(index, 1), :]).astype(jnp.bfloat16)
        low, high = normed[:, :half], normed[:, half:]
        kept_ref[index] = jnp.where(core == 0, low, high)
        given_ref[index] = jnp.where(core == 0, high, low)


def norm_tokens(place, gain, token_blocks):
    count, width = token_blocks[0].shape
    shape = jax.ShapeDtypeStruct((len(token_blocks), count, width // 2), jnp.bfloat16)
    return pl.pallas_call(
        norm_kernel,
        out_shape=(shape, shape),
        in_specs=[SMEM] + [VMEM] * (1 + len(token_blocks)),
        out_specs=(VMEM, VMEM),
        compiler_params=pltpu.CompilerParams(vmem_limit_bytes=8 << 20),
        name="norm_tokens",
    )(place, gain, *token_blocks)


def multiply_pieces(groups, held, pair, piece, width, own_refs, send_refs):
    blocks, tokens_two, _ = held.shape
    count = tokens_two // 2
    tile = min(256, width, held.shape[2])
    for group, own_ref, send_ref in zip(groups, own_refs, send_refs):
        for place, part in enumerate(group):
            for start in range(0, width, tile):
                stop = min(start + tile, width)
                total = None
                for step in range(blocks):
                    weight = piece(step, part, start, stop)
                    term = jnp.dot(held[pair ^ step], weight, preferred_element_type=jnp.float32)
                    total = term if total is None else total + term
                where = slice(place * width + start, place * width + stop)
                own_ref[:, where] = total[:count]
                send_ref[:, where] = total[count:].astype(send_ref.dtype)


def pack_kernel(qkv_ref, out_ref, packed_ref):
    parts, depth, width = qkv_ref.shape
    row = 0
    for part in range(parts):
        for start in range(0, width, depth):
            packed_ref[row : row + depth, :] = qkv_ref[part, :, start : start + depth]
            row += depth
    packed_ref[row:, :] = out_ref[...]


def packed(w_qkv, w_out):
    parts, depth, width = w_qkv.shape
    count = parts * width // depth
    return pl.pallas_call(
        pack_kernel,
        out_shape=jax.ShapeDtypeStruct((count * depth + width, depth), w_qkv.dtype),
        in_specs=[VMEM, VMEM],
        out_specs=VMEM,
        compiler_params=pltpu.CompilerParams(vmem_limit_bytes=8 << 20),
        name="pack",
    )(w_qkv, w_out)


def relay_kernel(low_in, high_in, low_ref, high_ref):
    half = low_ref.shape[0]
    low_ref[...] = low_in[:half]
    high_ref[...] = high_in[half:]


def relayed(near):
    if len(near) != 2:
        return []
    rows, width = near[0].shape
    shape = jax.ShapeDtypeStruct((rows // 2, width), near[0].dtype)
    return pl.pallas_call(
        relay_kernel,
        out_shape=(shape, shape),
        in_specs=[VMEM] * 2,
        out_specs=(VMEM, VMEM),
        compiler_params=pltpu.CompilerParams(vmem_limit_bytes=8 << 20),
        name="relay",
    )(*near)


def qkv_kernel(place_ref, own_in_ref, other_in_ref, *refs):
    *weight_refs, own_q, own_kv, send_q, send_kv, held = refs
    count = own_in_ref.shape[1]
    held[:, :count] = own_in_ref[...]
    held[:, count:] = other_in_ref[...]
    blocks, depth = held.shape[0], weight_refs[0].shape[1]
    direct = blocks - 1 if len(weight_refs) == blocks + 1 else blocks
    width = own_q.shape[1]

    def piece(step, part, start, stop):
        row = (part * width // depth + start // depth) * depth
        offset = start % depth
        if step < direct:
            return weight_refs[step][row : row + depth, offset : offset + stop - start]
        half = weight_refs[direct].shape[0]
        row = row - row // half * half
        which = (part * width + start) // (half // depth * depth)
        return weight_refs[direct + which][row : row + depth, offset : offset + stop - start]

    multiply_pieces(
        ((0,), (1, 2)), held, place_ref[0] // 2, piece, width, (own_q, own_kv), (send_q, send_kv)
    )


def project_qkv(place, own, other, pieces):
    blocks, count, depth = own.shape
    width = 2 * depth
    shapes = [jax.ShapeDtypeStruct((count, n * width), jnp.float32) for n in (1, 2)] * 2
    return pl.pallas_call(
        qkv_kernel,
        out_shape=tuple(shapes),
        in_specs=[SMEM] + [VMEM] * (2 + len(pieces)),
        out_specs=tuple([VMEM] * 4),
        scratch_shapes=[pltpu.VMEM((blocks, 2 * count, depth), jnp.bfloat16)],
        compiler_params=pltpu.CompilerParams(vmem_limit_bytes=16 << 20),
        cost_estimate=pl.CostEstimate(
            flops=12 * count * depth * blocks * width,
            bytes_accessed=6 * depth * blocks * width,
            transcendentals=0,
        ),
        name="qkv",
    )(place, own, other, *pieces)


def ffn_in_kernel(place_ref, gain_ref, *refs):
    blocks = lax.axis_size("col")
    block_refs, refs = refs[:blocks], refs[blocks:]
    *weight_refs, own_ref, send_ref, held = refs
    row, col = place_ref[0], place_ref[1]
    for step, ref in enumerate(block_refs):
        index = lax.rem(col - step + blocks, blocks)
        gain = gain_ref[pl.ds(2 * index + lax.rem(row, 2), 1), :]
        held[index] = (ref[...].astype(jnp.float32) * gain).astype(jnp.bfloat16)
    def piece(step, part, start, stop):
        return half_ref(weight_refs, step, part)[:, start:stop]

    width = weight_refs[0].shape[2]
    multiply_pieces(((0, 1),), held, row // 2, piece, width, (own_ref,), (send_ref,))


def project_ffn(place, gain, token_blocks, pieces):
    tokens_two, depth = token_blocks[0].shape
    blocks, count = len(token_blocks), tokens_two // 2
    columns = 2 * pieces[0].shape[2]
    return pl.pallas_call(
        ffn_in_kernel,
        out_shape=(
            jax.ShapeDtypeStruct((count, columns), jnp.float32),
            jax.ShapeDtypeStruct((count, columns), jnp.bfloat16),
        ),
        in_specs=[SMEM] + [VMEM] * (1 + blocks + len(pieces)),
        out_specs=(VMEM, VMEM),
        scratch_shapes=[pltpu.VMEM((blocks, tokens_two, depth), jnp.bfloat16)],
        compiler_params=pltpu.CompilerParams(vmem_limit_bytes=16 << 20),
        cost_estimate=pl.CostEstimate(
            flops=2 * tokens_two * depth * blocks * columns,
            bytes_accessed=2 * depth * blocks * columns,
            transcendentals=0,
        ),
        name="ffn_in",
    )(place, gain, *token_blocks, *pieces)


def columns_kernel(first, place_ref, own_in_ref, other_in_ref, *refs):
    blocks = lax.axis_size("col")
    *weight_refs, own_ref = refs[: len(refs) - blocks]
    send_refs, held = refs[len(refs) - blocks : -1], refs[-1]
    row, col = place_ref[0], place_ref[1]
    pair = row // 2
    hidden = jnp.concatenate([own_in_ref[...], other_in_ref[...]], axis=0)
    far = len(weight_refs) == blocks + 1
    direct = blocks - 1 if far else blocks
    for step in range(blocks):
        if not first:
            half = hidden.shape[1] // 2
            total = jnp.dot(
                hidden[:, :half],
                half_ref(weight_refs, step, 0)[...],
                preferred_element_type=jnp.float32,
            ) + jnp.dot(
                hidden[:, half:],
                half_ref(weight_refs, step, 1)[...],
                preferred_element_type=jnp.float32,
            )
        elif step < direct:
            total = jnp.dot(hidden, weight_refs[step][first:, :], preferred_element_type=jnp.float32)
        else:
            skipped = first - weight_refs[direct].shape[0]
            total = jnp.dot(
                hidden, weight_refs[direct + 1][skipped:, :], preferred_element_type=jnp.float32
            )
        held[lax.rem((pair ^ step) - col + blocks, blocks)] = total
    own_ref[...] = held[0]
    for step in range(1, blocks):
        send_refs[step - 1][...] = held[step].astype(jnp.bfloat16)


def columns(place, own, other, pieces, name):
    count, depth = own.shape
    width = pieces[0].shape[-1]
    blocks = lax.axis_size("col")
    return pl.pallas_call(
        functools.partial(columns_kernel, pieces[0].size // width - depth),
        out_shape=(
            jax.ShapeDtypeStruct((2 * count, width), jnp.float32),
            *[jax.ShapeDtypeStruct((2 * count, width), jnp.bfloat16)] * (blocks - 1),
        ),
        in_specs=[SMEM] + [VMEM] * (2 + len(pieces)),
        out_specs=tuple([VMEM] * blocks),
        scratch_shapes=[pltpu.VMEM((blocks, 2 * count, width), jnp.float32)],
        compiler_params=pltpu.CompilerParams(vmem_limit_bytes=16 << 20),
        cost_estimate=pl.CostEstimate(
            flops=4 * count * depth * width * blocks,
            bytes_accessed=2 * depth * width * blocks,
            transcendentals=0,
        ),
        name=name,
    )(place, own, other, *pieces)


def summed(own, sends, residual):
    total = own + residual.astype(jnp.float32)
    for step, send in enumerate(sends, 1):
        total = total + shifted(send, step).astype(jnp.float32)
    return total.astype(jnp.bfloat16)


def gathered(block):
    return [block] + [shifted(block, step) for step in range(1, lax.axis_size("col"))]


def square_sums(blocks):
    return sum(jnp.sum(jnp.square(b.astype(jnp.float32)), axis=1) for b in blocks)


def per_device(
    tokens,
    segment_ids,
    bucket_table,
    slot_index,
    gain_attn,
    w_qkv,
    rel_bias,
    w_out,
    gain_ffn,
    w_in,
    w_down,
):
    rows, cols = lax.axis_size("row"), lax.axis_size("col")
    count, width = tokens.shape
    half = width // 2
    features = width * cols
    row, col = lax.axis_index("row"), lax.axis_index("col")
    core = row % 2
    place = jnp.stack([row, col]).astype(jnp.int32)

    first = packed(w_qkv, w_out)
    first_near = near_pieces(first)
    token_blocks = gathered(tokens)
    kept, given = norm_tokens(place, gain_attn.reshape(cols, width), token_blocks)
    received = other_core(after(given, *first_near))
    token_block = jnp.concatenate(
        [
            jnp.where(core == 0, tokens[:, :half], tokens[:, half:]),
            other_core(jnp.where(core == 0, tokens[:, half:], tokens[:, :half])),
        ],
        axis=0,
    )
    bias = masked_bias(row, segment_ids, bucket_table, rel_bias, count)
    first_far = [pair_exchange(p, step) for p, step in zip(relayed(first_near), (2, 1))]
    first_pieces = [first, *first_near, *first_far]
    kept, bias, token_block = lax.optimization_barrier((kept, bias, token_block))
    w_in, w_down, *_ = lax.optimization_barrier((w_in, w_down.reshape(2, -1, half), received))
    down_first = first_phase(w_down[0], w_down[1])
    in_first = first_phase(w_in[0], w_in[1])
    own_q, own_kv, send_q, send_kv = project_qkv(
        place, kept, received, first_pieces
    )
    other_kv, *down_first = lax.optimization_barrier((other_core(send_kv), *down_first))
    key_value = (own_kv + other_kv).astype(jnp.bfloat16)
    queries = (own_q + other_core(after(send_q, key_value))).astype(jnp.bfloat16)
    forward = [(i, i + 1) for i in range(rows - 1)]
    backward = [(target, source) for source, target in forward]
    low = lax.ppermute(key_value, "row", forward)
    high = lax.ppermute(key_value, "row", backward)
    low, high, *in_first = lax.optimization_barrier((low, high, *in_first))
    in_pieces = [w_in, *in_first, *second_phase(w_in, in_first)]
    context = attention(queries, low, key_value, high, bias)
    own, *sends = columns(
        place, context, other_core(context), first_pieces, "attention_out"
    )
    middle = summed(own, sends, token_block)

    middle_blocks = gathered(middle)
    squares = square_sums(middle_blocks)
    squares = squares[:count] + other_core(squares[count:])
    scale = lax.rsqrt(squares / features + epsilon)[:, None]
    down_second = second_phase(after(w_down, middle_blocks[-1]), down_first)
    own, send = project_ffn(
        place, gain_ffn.reshape(rows, -1), middle_blocks, in_pieces
    )
    other_sum, *down_second = lax.optimization_barrier((other_core(send), *down_second))
    branches = (own + other_sum.astype(jnp.float32)) * scale
    inner = branches.shape[1] // 2
    hidden = (
        jax.nn.gelu(branches[:, :inner], approximate=True) * branches[:, inner:]
    ).astype(jnp.bfloat16)
    own, *sends = columns(
        place, hidden, other_core(hidden), [w_down, *down_first, *down_second], "ffn_out"
    )
    result = summed(own, sends, middle)
    received = other_core(result[count:])
    output = jnp.where(
        core == 0,
        jnp.concatenate([result[:count], received], axis=1),
        jnp.concatenate([received, result[:count]], axis=1),
    )

    stacked = jnp.stack([key_value[:, :width], key_value[:, width:]])
    blocks = stacked.reshape(2, slot_index.shape[1], BLOCK, width)
    kv_cache = (
        jnp.zeros_like(blocks).at[:, slot_index[0]].set(blocks).reshape(2, count, width)
    )
    return (output, kv_cache)


def solution(mesh):
    return jax.shard_map(
        per_device,
        mesh=mesh,
        in_specs=(
            P("row", "col"),
            P(),
            P(),
            P("row", None),
            P(),
            P(None, "row", "col"),
            P(None, "col"),
            P("col", "row"),
            P(),
            P(None, "row", "col"),
            P("col", "row"),
        ),
        out_specs=(P("row", "col"), P(None, "row", "col")),
        check_vma=False,
    )
```

```python
import functools

import jax
import jax.numpy as jnp
from jax import lax
from jax.experimental import pallas as pl
from jax.experimental.pallas import tpu as pltpu
from jax.sharding import PartitionSpec as P

BLOCK = 128


epsilon = 1e-06
masked_score = -1e30
VMEM = pl.BlockSpec(memory_space=pltpu.VMEM)
SMEM = pl.BlockSpec(memory_space=pltpu.SMEM)


def bias_kernel(row_ref, seg_ref, table_ref, rel_ref, out_ref):
    heads, count, width = out_ref.shape
    rows = seg_ref.shape[0]
    row = row_ref[0]
    table = table_ref[...]
    rel = rel_ref[...]
    by_distance = jnp.zeros((heads, table.shape[1]), jnp.float32)
    for bucket in range(rel.shape[1]):
        by_distance = jnp.where(table == bucket, rel[:, bucket : bucket + 1], by_distance)
    by_distance = jnp.concatenate(
        [by_distance, jnp.zeros((heads, width - table.shape[1]), jnp.float32)], axis=1
    )

    def segment_row(index):
        clipped = jnp.clip(index, 0, rows - 1)
        found = seg_ref[pl.ds(clipped, 1), :].astype(jnp.float32)
        return jnp.where(index == clipped, found, -1.0)

    own = segment_row(row)
    query_seg = jnp.broadcast_to(own, (count, count)).T
    allowed = jnp.concatenate(
        [query_seg == segment_row(row - 1), query_seg == own, query_seg == segment_row(row + 1)],
        axis=1,
    )
    for head in range(heads):
        line = jnp.broadcast_to(by_distance[head : head + 1, :], (count, width))
        shifted = pltpu.roll(line, 1, 1, stride=1, stride_axis=0)
        out_ref[head] = jnp.where(allowed, shifted, masked_score)


def masked_bias(row, segment_ids, bucket_table, rel_bias, count):
    heads = rel_bias.shape[1]
    table = jnp.pad(bucket_table, (0, 1)).reshape(1, 2 * count)
    return pl.pallas_call(
        bias_kernel,
        out_shape=jax.ShapeDtypeStruct((heads, count, 3 * count), jnp.float32),
        in_specs=[SMEM, VMEM, VMEM, VMEM],
        out_specs=VMEM,
        compiler_params=pltpu.CompilerParams(vmem_limit_bytes=8 << 20),
        name="masked_bias",
    )(row.reshape(1), segment_ids.reshape(-1, count), table, rel_bias.T)


def attention_kernel(q_ref, low_ref, own_ref, high_ref, bias_ref, out_ref):
    heads, count, _ = bias_ref.shape
    total_width = q_ref.shape[1]
    width = total_width // heads
    sides = (low_ref, own_ref, high_ref)
    for pair in range(0, heads, 2):
        parts = []
        for head in (pair, pair + 1):
            cut = slice(head * width, (head + 1) * width)
            after_keys = slice(total_width + head * width, total_width + (head + 1) * width)
            query = q_ref[:, cut]
            scores = jnp.concatenate(
                [
                    lax.dot_general(
                        query,
                        ref[:, cut],
                        (((1,), (1,)), ((), ())),
                        preferred_element_type=jnp.float32,
                    )
                    for ref in sides
                ],
                axis=1,
            )
            scores = scores + bias_ref[head]
            top = jnp.max(scores, axis=1, keepdims=True)
            weights = jnp.exp(scores - top)
            denominator = jnp.sum(weights, axis=1, keepdims=True)
            rounded = weights.astype(jnp.bfloat16)
            total = sum(
                jnp.dot(
                    rounded[:, i * count : (i + 1) * count],
                    ref[:, after_keys],
                    preferred_element_type=jnp.float32,
                )
                for i, ref in enumerate(sides)
            )
            parts.append(total / denominator)
        out_ref[:, pair * width : (pair + 2) * width] = jnp.concatenate(parts, axis=1).astype(
            out_ref.dtype
        )


def attention(queries, low, own, high, bias):
    count, span = bias.shape[1:]
    return pl.pallas_call(
        attention_kernel,
        out_shape=jax.ShapeDtypeStruct(queries.shape, jnp.bfloat16),
        in_specs=[VMEM] * 5,
        out_specs=VMEM,
        compiler_params=pltpu.CompilerParams(vmem_limit_bytes=8 << 20),
        cost_estimate=pl.CostEstimate(
            flops=4 * queries.size * span, bytes_accessed=4 * bias.size, transcendentals=bias.size
        ),
        name="attention",
    )(queries, low, own, high, bias)


def exchange(value, axis, partner):
    count = lax.axis_size(axis)
    return lax.ppermute(value, axis, [(i, partner(i) % count) for i in range(count)])


def other_core(value):
    return exchange(value, "row", lambda i: i ^ 1)


def pair_exchange(value, step):
    return exchange(value, "row", lambda i: i ^ (2 * step))


def shifted(value, step):
    return exchange(value, "col", lambda i: i + step)


def after(value, *earlier):
    return lax.optimization_barrier((value, *earlier))[0]


def near_pieces(weight):
    pairs = lax.axis_size("row") // 2
    if pairs == 4:
        return [pair_exchange(weight, 1), pair_exchange(weight, 2)]
    return [pair_exchange(weight, step) for step in range(1, pairs)]


def after_all(values, *earlier):
    return list(lax.optimization_barrier((*values, *earlier))[: len(values)])


def first_hop(weight, *earlier):
    weight = after(weight, *earlier)
    return weight, near_pieces(weight)


def first_phase(low, high):
    pairs = lax.axis_size("row") // 2
    if pairs != 4:
        return [pair_exchange(part, step) for step in range(1, pairs) for part in (low, high)]
    return [pair_exchange(low, 1), pair_exchange(high, 2)]


def packet_kernel(own_ref, low_in, high_in, low_ref, high_ref):
    size = low_in.shape[0]
    low_ref[0], high_ref[0] = own_ref[0], own_ref[1]
    low_ref[1], high_ref[1] = low_in[...], high_in[...]


def second_phase(own, first):
    if len(first) != 2:
        return []
    shape = jax.ShapeDtypeStruct(own.shape, own.dtype)
    low, high = pl.pallas_call(
        packet_kernel,
        out_shape=(shape, shape),
        in_specs=[VMEM] * 3,
        out_specs=(VMEM, VMEM),
        compiler_params=pltpu.CompilerParams(vmem_limit_bytes=8 << 20),
        name="packet",
    )(own, *first)
    return [pair_exchange(high, 1), pair_exchange(low, 2)]


def half_ref(refs, step, part):
    own, *others = refs
    if step == 0:
        return own.at[part]
    if len(others) != 4:
        return others[2 * (step - 1) + part]
    near_low, side_high, highs, lows = others
    if step == 3:
        return (highs if part else lows).at[1]
    if part == step - 1:
        return near_low if part == 0 else side_high
    return (highs if part else lows).at[0]


def norm_kernel(place_ref, gain_ref, *refs):
    *block_refs, kept_ref, given_ref = refs
    blocks = len(block_refs)
    core, col = lax.rem(place_ref[0], 2), place_ref[1]
    wide = [ref[...].astype(jnp.float32) for ref in block_refs]
    squares = sum(jnp.sum(block * block, axis=1, keepdims=True) for block in wide)
    half = wide[0].shape[1] // 2
    scale = lax.rsqrt(squares / (2 * half * blocks) + epsilon)
    for step, block in enumerate(wide):
        index = lax.rem(col - step + blocks, blocks)
        normed = (block * scale * gain_ref[pl.ds(index, 1), :]).astype(jnp.bfloat16)
        low, high = normed[:, :half], normed[:, half:]
        kept_ref[index] = jnp.where(core == 0, low, high)
        given_ref[index] = jnp.where(core == 0, high, low)


def norm_tokens(place, gain, token_blocks):
    count, width = token_blocks[0].shape
    shape = jax.ShapeDtypeStruct((len(token_blocks), count, width // 2), jnp.bfloat16)
    return pl.pallas_call(
        norm_kernel,
        out_shape=(shape, shape),
        in_specs=[SMEM] + [VMEM] * (1 + len(token_blocks)),
        out_specs=(VMEM, VMEM),
        compiler_params=pltpu.CompilerParams(vmem_limit_bytes=8 << 20),
        name="norm_tokens",
    )(place, gain, *token_blocks)


def multiply_pieces(groups, held, pair, piece, width, own_refs, send_refs):
    blocks, tokens_two, _ = held.shape
    count = tokens_two // 2
    tile = min(256, width, held.shape[2])
    for group, own_ref, send_ref in zip(groups, own_refs, send_refs):
        for place, part in enumerate(group):
            for start in range(0, width, tile):
                stop = min(start + tile, width)
                total = None
                for step in range(blocks):
                    weight = piece(step, part, start, stop)
                    term = jnp.dot(held[pair ^ step], weight, preferred_element_type=jnp.float32)
                    total = term if total is None else total + term
                where = slice(place * width + start, place * width + stop)
                own_ref[:, where] = total[:count]
                send_ref[:, where] = total[count:].astype(send_ref.dtype)


def relay_kernel(qkv_low, qkv_high, out_low, out_high, low_ref, high_ref):
    half = low_ref.shape[2]
    parts = qkv_low.shape[0]
    low_ref[:parts] = qkv_low[:, :, :half]
    low_ref[parts] = out_low[:half]
    high_ref[:parts] = qkv_high[:, :, half:]
    high_ref[parts] = out_high[half:]


def relayed(qkv_near, out_near):
    if len(qkv_near) != 2:
        return []
    parts, depth, _ = qkv_near[0].shape
    shape = jax.ShapeDtypeStruct((parts + 1, depth, depth), qkv_near[0].dtype)
    low, high = pl.pallas_call(
        relay_kernel,
        out_shape=(shape, shape),
        in_specs=[VMEM] * 4,
        out_specs=(VMEM, VMEM),
        compiler_params=pltpu.CompilerParams(vmem_limit_bytes=8 << 20),
        name="relay",
    )(*qkv_near, *out_near)
    return [pair_exchange(low, 2), pair_exchange(high, 1)]


def qkv_kernel(place_ref, own_in_ref, other_in_ref, *refs):
    *weight_refs, own_q, own_kv, send_q, send_kv, held = refs
    count = own_in_ref.shape[1]
    held[:, :count] = own_in_ref[...]
    held[:, count:] = other_in_ref[...]
    blocks, width = held.shape[0], own_q.shape[1]
    direct = blocks - 1 if len(weight_refs) == blocks + 1 else blocks

    def piece(step, part, start, stop):
        if step < direct:
            return weight_refs[step][part, :, start:stop]
        half = start // (width // 2)
        offset = start - half * (width // 2)
        return weight_refs[direct + half][part, :, offset : offset + stop - start]

    multiply_pieces(
        ((0,), (1, 2)), held, place_ref[0] // 2, piece, width, (own_q, own_kv), (send_q, send_kv)
    )


def project_qkv(place, own, other, pieces):
    blocks, count, depth = own.shape
    width = 2 * depth
    shapes = [jax.ShapeDtypeStruct((count, n * width), jnp.float32) for n in (1, 2)] * 2
    return pl.pallas_call(
        qkv_kernel,
        out_shape=tuple(shapes),
        in_specs=[SMEM] + [VMEM] * (2 + len(pieces)),
        out_specs=tuple([VMEM] * 4),
        scratch_shapes=[pltpu.VMEM((blocks, 2 * count, depth), jnp.bfloat16)],
        compiler_params=pltpu.CompilerParams(vmem_limit_bytes=8 << 20),
        cost_estimate=pl.CostEstimate(
            flops=12 * count * depth * blocks * width,
            bytes_accessed=6 * depth * blocks * width,
            transcendentals=0,
        ),
        name="qkv",
    )(place, own, other, *pieces)


def ffn_in_kernel(place_ref, gain_ref, *refs):
    blocks = lax.axis_size("col")
    block_refs, refs = refs[:blocks], refs[blocks:]
    *weight_refs, own_ref, send_ref, held = refs
    row, col = place_ref[0], place_ref[1]
    for step, ref in enumerate(block_refs):
        index = lax.rem(col - step + blocks, blocks)
        gain = gain_ref[pl.ds(2 * index + lax.rem(row, 2), 1), :]
        held[index] = (ref[...].astype(jnp.float32) * gain).astype(jnp.bfloat16)
    def piece(step, part, start, stop):
        return half_ref(weight_refs, step, part)[:, start:stop]

    width = weight_refs[0].shape[2]
    multiply_pieces(((0, 1),), held, row // 2, piece, width, (own_ref,), (send_ref,))


def project_ffn(place, gain, token_blocks, pieces):
    tokens_two, depth = token_blocks[0].shape
    blocks, count = len(token_blocks), tokens_two // 2
    columns = 2 * pieces[0].shape[2]
    return pl.pallas_call(
        ffn_in_kernel,
        out_shape=(
            jax.ShapeDtypeStruct((count, columns), jnp.float32),
            jax.ShapeDtypeStruct((count, columns), jnp.bfloat16),
        ),
        in_specs=[SMEM] + [VMEM] * (1 + blocks + len(pieces)),
        out_specs=(VMEM, VMEM),
        scratch_shapes=[pltpu.VMEM((blocks, tokens_two, depth), jnp.bfloat16)],
        compiler_params=pltpu.CompilerParams(vmem_limit_bytes=8 << 20),
        cost_estimate=pl.CostEstimate(
            flops=2 * tokens_two * depth * blocks * columns,
            bytes_accessed=2 * depth * blocks * columns,
            transcendentals=0,
        ),
        name="ffn_in",
    )(place, gain, *token_blocks, *pieces)


def columns_kernel(place_ref, own_in_ref, other_in_ref, *refs):
    blocks = lax.axis_size("col")
    *weight_refs, own_ref = refs[: len(refs) - blocks]
    send_refs, held = refs[len(refs) - blocks : -1], refs[-1]
    row, col = place_ref[0], place_ref[1]
    pair = row // 2
    hidden = jnp.concatenate([own_in_ref[...], other_in_ref[...]], axis=0)
    far = len(weight_refs) == blocks + 1
    direct = blocks - 1 if far else blocks
    for step in range(blocks):
        if len(weight_refs[0].shape) == 3:
            half = hidden.shape[1] // 2
            total = jnp.dot(
                hidden[:, :half],
                half_ref(weight_refs, step, 0)[...],
                preferred_element_type=jnp.float32,
            ) + jnp.dot(
                hidden[:, half:],
                half_ref(weight_refs, step, 1)[...],
                preferred_element_type=jnp.float32,
            )
        elif step < direct:
            total = jnp.dot(hidden, weight_refs[step][...], preferred_element_type=jnp.float32)
        else:
            half = hidden.shape[1] // 2
            low, high = (ref[ref.shape[0] - 1] for ref in weight_refs[direct:])
            total = jnp.dot(
                hidden[:, :half], low, preferred_element_type=jnp.float32
            ) + jnp.dot(hidden[:, half:], high, preferred_element_type=jnp.float32)
        held[lax.rem((pair ^ step) - col + blocks, blocks)] = total
    own_ref[...] = held[0]
    for step in range(1, blocks):
        send_refs[step - 1][...] = held[step].astype(jnp.bfloat16)


def columns(place, own, other, pieces, name):
    count, depth = own.shape
    width = pieces[0].shape[-1]
    blocks = lax.axis_size("col")
    return pl.pallas_call(
        columns_kernel,
        out_shape=(
            jax.ShapeDtypeStruct((2 * count, width), jnp.float32),
            *[jax.ShapeDtypeStruct((2 * count, width), jnp.bfloat16)] * (blocks - 1),
        ),
        in_specs=[SMEM] + [VMEM] * (2 + len(pieces)),
        out_specs=tuple([VMEM] * blocks),
        scratch_shapes=[pltpu.VMEM((blocks, 2 * count, width), jnp.float32)],
        compiler_params=pltpu.CompilerParams(vmem_limit_bytes=8 << 20),
        cost_estimate=pl.CostEstimate(
            flops=4 * count * depth * width * blocks,
            bytes_accessed=2 * depth * width * blocks,
            transcendentals=0,
        ),
        name=name,
    )(place, own, other, *pieces)


def summed(own, sends, residual):
    total = own + residual.astype(jnp.float32)
    for step, send in enumerate(sends, 1):
        total = total + shifted(send, step).astype(jnp.float32)
    return total.astype(jnp.bfloat16)


def gathered(block):
    return [block] + [shifted(block, step) for step in range(1, lax.axis_size("col"))]


def square_sums(blocks):
    return sum(jnp.sum(jnp.square(b.astype(jnp.float32)), axis=1) for b in blocks)


def per_device(
    tokens,
    segment_ids,
    bucket_table,
    slot_index,
    gain_attn,
    w_qkv,
    rel_bias,
    w_out,
    gain_ffn,
    w_in,
    w_down,
):
    rows, cols = lax.axis_size("row"), lax.axis_size("col")
    count, width = tokens.shape
    half = width // 2
    features = width * cols
    row, col = lax.axis_index("row"), lax.axis_index("col")
    core = row % 2
    place = jnp.stack([row, col]).astype(jnp.int32)

    qkv_near = near_pieces(w_qkv)
    token_blocks = gathered(tokens)
    kept, given = norm_tokens(place, gain_attn.reshape(cols, width), token_blocks)
    out_near = near_pieces(after(w_out, token_blocks[1]))
    token_block = jnp.concatenate(
        [
            jnp.where(core == 0, tokens[:, :half], tokens[:, half:]),
            other_core(jnp.where(core == 0, tokens[:, half:], tokens[:, :half])),
        ],
        axis=0,
    )
    bias = masked_bias(row, segment_ids, bucket_table, rel_bias, count)
    ready = lax.optimization_barrier((*qkv_near, *out_near, kept, given, bias, token_block))
    *near, kept, given, bias, token_block = ready
    received = other_core(given)
    qkv_near, out_near = near[: len(near) // 2], near[len(near) // 2 :]
    far = relayed(qkv_near, out_near)
    w_in, w_down, *_ = lax.optimization_barrier((w_in, w_down.reshape(2, -1, half), received))
    down_first = first_phase(w_down[0], w_down[1])
    in_first = first_phase(w_in[0], w_in[1])
    own_q, own_kv, send_q, send_kv = project_qkv(
        place, kept, received, [w_qkv, *qkv_near, *far]
    )
    other_kv, other_q, *down_first = lax.optimization_barrier(
        (other_core(send_kv), other_core(send_q), *down_first)
    )
    key_value = (own_kv + other_kv).astype(jnp.bfloat16)
    queries = (own_q + other_q).astype(jnp.bfloat16)
    forward = [(i, i + 1) for i in range(rows - 1)]
    backward = [(target, source) for source, target in forward]
    low = lax.ppermute(key_value, "row", forward)
    high = lax.ppermute(key_value, "row", backward)
    low, high, *in_first = lax.optimization_barrier((low, high, *in_first))
    in_pieces = [w_in, *in_first, *second_phase(w_in, in_first)]
    context = attention(queries, low, key_value, high, bias)
    own, *sends = columns(
        place, context, other_core(context), [w_out, *out_near, *far], "attention_out"
    )
    stacked = jnp.stack([key_value[:, :width], key_value[:, width:]])
    blocks = stacked.reshape(2, slot_index.shape[1], BLOCK, width)
    kv_cache = (
        jnp.zeros_like(blocks).at[:, slot_index[0]].set(blocks).reshape(2, count, width)
    )
    middle, kv_cache = lax.optimization_barrier((summed(own, sends, token_block), kv_cache))

    middle_blocks = gathered(middle)
    squares = square_sums(middle_blocks)
    squares = squares[:count] + other_core(squares[count:])
    scale = lax.rsqrt(squares / features + epsilon)[:, None]
    down_second = second_phase(after(w_down, middle_blocks[-1]), down_first)
    own, send = project_ffn(
        place, gain_ffn.reshape(rows, -1), middle_blocks, in_pieces
    )
    other_sum, *down_second = lax.optimization_barrier((other_core(send), *down_second))
    branches = (own + other_sum.astype(jnp.float32)) * scale
    inner = branches.shape[1] // 2
    hidden = (
        jax.nn.gelu(branches[:, :inner], approximate=True) * branches[:, inner:]
    ).astype(jnp.bfloat16)
    own, *sends = columns(
        place, hidden, other_core(hidden), [w_down, *down_first, *down_second], "ffn_out"
    )
    result = summed(own, sends, middle)
    received = other_core(result[count:])
    output = jnp.where(
        core == 0,
        jnp.concatenate([result[:count], received], axis=1),
        jnp.concatenate([received, result[:count]], axis=1),
    )

    return (output, kv_cache)


def solution(mesh):
    return jax.shard_map(
        per_device,
        mesh=mesh,
        in_specs=(
            P("row", "col"),
            P(),
            P(),
            P("row", None),
            P(),
            P(None, "row", "col"),
            P(None, "col"),
            P("col", "row"),
            P(),
            P(None, "row", "col"),
            P("col", "row"),
        ),
        out_specs=(P("row", "col"), P(None, "row", "col")),
        check_vma=False,
    )
```

```python
import functools

import jax
import jax.numpy as jnp
from jax import lax
from jax.experimental import pallas as pl
from jax.experimental.pallas import tpu as pltpu
from jax.sharding import PartitionSpec as P

BLOCK = 128


epsilon = 1e-06
masked_score = -1e30
VMEM = pl.BlockSpec(memory_space=pltpu.VMEM)
SMEM = pl.BlockSpec(memory_space=pltpu.SMEM)


def bias_kernel(row_ref, seg_ref, table_ref, rel_ref, out_ref):
    heads, count, width = out_ref.shape
    rows = seg_ref.shape[0]
    row = row_ref[0]
    table = table_ref[...]
    rel = rel_ref[...]
    by_distance = jnp.zeros((heads, table.shape[1]), jnp.float32)
    for bucket in range(rel.shape[1]):
        by_distance = jnp.where(table == bucket, rel[:, bucket : bucket + 1], by_distance)
    by_distance = jnp.concatenate(
        [by_distance, jnp.zeros((heads, width - table.shape[1]), jnp.float32)], axis=1
    )

    def segment_row(index):
        clipped = jnp.clip(index, 0, rows - 1)
        found = seg_ref[pl.ds(clipped, 1), :].astype(jnp.float32)
        return jnp.where(index == clipped, found, -1.0)

    own = segment_row(row)
    query_seg = jnp.broadcast_to(own, (count, count)).T
    allowed = jnp.concatenate(
        [query_seg == segment_row(row - 1), query_seg == own, query_seg == segment_row(row + 1)],
        axis=1,
    )
    for head in range(heads):
        line = jnp.broadcast_to(by_distance[head : head + 1, :], (count, width))
        shifted = pltpu.roll(line, 1, 1, stride=1, stride_axis=0)
        out_ref[head] = jnp.where(allowed, shifted, masked_score)


def masked_bias(row, segment_ids, bucket_table, rel_bias, count):
    heads = rel_bias.shape[1]
    table = jnp.pad(bucket_table, (0, 1)).reshape(1, 2 * count)
    return pl.pallas_call(
        bias_kernel,
        out_shape=jax.ShapeDtypeStruct((heads, count, 3 * count), jnp.float32),
        in_specs=[SMEM, VMEM, VMEM, VMEM],
        out_specs=VMEM,
        compiler_params=pltpu.CompilerParams(vmem_limit_bytes=8 << 20),
        name="masked_bias",
    )(row.reshape(1), segment_ids.reshape(-1, count), table, rel_bias.T)


def attention_kernel(q_ref, low_ref, own_ref, high_ref, bias_ref, out_ref):
    heads, count, _ = bias_ref.shape
    total_width = q_ref.shape[1]
    width = total_width // heads
    sides = (low_ref, own_ref, high_ref)
    for pair in range(0, heads, 2):
        parts = []
        for head in (pair, pair + 1):
            cut = slice(head * width, (head + 1) * width)
            after_keys = slice(total_width + head * width, total_width + (head + 1) * width)
            query = q_ref[:, cut]
            scores = jnp.concatenate(
                [
                    lax.dot_general(
                        query,
                        ref[:, cut],
                        (((1,), (1,)), ((), ())),
                        preferred_element_type=jnp.float32,
                    )
                    for ref in sides
                ],
                axis=1,
            )
            scores = scores + bias_ref[head]
            top = jnp.max(scores, axis=1, keepdims=True)
            weights = jnp.exp(scores - top)
            denominator = jnp.sum(weights, axis=1, keepdims=True)
            rounded = weights.astype(jnp.bfloat16)
            total = sum(
                jnp.dot(
                    rounded[:, i * count : (i + 1) * count],
                    ref[:, after_keys],
                    preferred_element_type=jnp.float32,
                )
                for i, ref in enumerate(sides)
            )
            parts.append(total / denominator)
        out_ref[:, pair * width : (pair + 2) * width] = jnp.concatenate(parts, axis=1).astype(
            out_ref.dtype
        )


def attention(queries, low, own, high, bias):
    count, span = bias.shape[1:]
    return pl.pallas_call(
        attention_kernel,
        out_shape=jax.ShapeDtypeStruct(queries.shape, jnp.bfloat16),
        in_specs=[VMEM] * 5,
        out_specs=VMEM,
        compiler_params=pltpu.CompilerParams(vmem_limit_bytes=8 << 20),
        cost_estimate=pl.CostEstimate(
            flops=4 * queries.size * span, bytes_accessed=4 * bias.size, transcendentals=bias.size
        ),
        name="attention",
    )(queries, low, own, high, bias)


def exchange(value, axis, partner):
    count = lax.axis_size(axis)
    return lax.ppermute(value, axis, [(i, partner(i) % count) for i in range(count)])


def other_core(value):
    return exchange(value, "row", lambda i: i ^ 1)


def pair_exchange(value, step):
    return exchange(value, "row", lambda i: i ^ (2 * step))


def shifted(value, step):
    return exchange(value, "col", lambda i: i + step)


def after(value, *earlier):
    return lax.optimization_barrier((value, *earlier))[0]


def near_pieces(weight):
    pairs = lax.axis_size("row") // 2
    if pairs == 4:
        return [pair_exchange(weight, 1), pair_exchange(weight, 2)]
    return [pair_exchange(weight, step) for step in range(1, pairs)]


def after_all(values, *earlier):
    return list(lax.optimization_barrier((*values, *earlier))[: len(values)])


def first_hop(weight, *earlier):
    weight = after(weight, *earlier)
    return weight, near_pieces(weight)


def first_phase(low, high):
    pairs = lax.axis_size("row") // 2
    if pairs != 4:
        return [pair_exchange(part, step) for step in range(1, pairs) for part in (low, high)]
    return [pair_exchange(low, 1), pair_exchange(high, 2)]


def packet_kernel(own_ref, low_in, high_in, low_ref, high_ref):
    size = low_in.shape[0]
    low_ref[0], high_ref[0] = own_ref[0], own_ref[1]
    low_ref[1], high_ref[1] = low_in[...], high_in[...]


def second_phase(own, first):
    if len(first) != 2:
        return []
    shape = jax.ShapeDtypeStruct(own.shape, own.dtype)
    low, high = pl.pallas_call(
        packet_kernel,
        out_shape=(shape, shape),
        in_specs=[VMEM] * 3,
        out_specs=(VMEM, VMEM),
        compiler_params=pltpu.CompilerParams(vmem_limit_bytes=8 << 20),
        name="packet",
    )(own, *first)
    return [low, high]


def exchanged(packets):
    return [pair_exchange(packet, step) for packet, step in zip(packets[::-1], (1, 2))]


def half_ref(refs, step, part):
    own, *others = refs
    if step == 0:
        return own.at[part]
    if len(others) != 4:
        return others[2 * (step - 1) + part]
    near_low, side_high, highs, lows = others
    if step == 3:
        return (highs if part else lows).at[1]
    if part == step - 1:
        return near_low if part == 0 else side_high
    return (highs if part else lows).at[0]


def norm_kernel(place_ref, gain_ref, *refs):
    *block_refs, kept_ref, given_ref = refs
    blocks = len(block_refs)
    core, col = lax.rem(place_ref[0], 2), place_ref[1]
    wide = [ref[...].astype(jnp.float32) for ref in block_refs]
    squares = sum(jnp.sum(block * block, axis=1, keepdims=True) for block in wide)
    half = wide[0].shape[1] // 2
    scale = lax.rsqrt(squares / (2 * half * blocks) + epsilon)
    for step, block in enumerate(wide):
        index = lax.rem(col - step + blocks, blocks)
        normed = (block * scale * gain_ref[pl.ds(index, 1), :]).astype(jnp.bfloat16)
        low, high = normed[:, :half], normed[:, half:]
        kept_ref[index] = jnp.where(core == 0, low, high)
        given_ref[index] = jnp.where(core == 0, high, low)


def norm_tokens(place, gain, token_blocks):
    count, width = token_blocks[0].shape
    shape = jax.ShapeDtypeStruct((len(token_blocks), count, width // 2), jnp.bfloat16)
    return pl.pallas_call(
        norm_kernel,
        out_shape=(shape, shape),
        in_specs=[SMEM] + [VMEM] * (1 + len(token_blocks)),
        out_specs=(VMEM, VMEM),
        compiler_params=pltpu.CompilerParams(vmem_limit_bytes=8 << 20),
        name="norm_tokens",
    )(place, gain, *token_blocks)


def multiply_pieces(groups, held, pair, piece, width, own_refs, send_refs):
    blocks, tokens_two, _ = held.shape
    count = tokens_two // 2
    tile = min(256, width, held.shape[2])
    for group, own_ref, send_ref in zip(groups, own_refs, send_refs):
        for place, part in enumerate(group):
            for start in range(0, width, tile):
                stop = min(start + tile, width)
                total = None
                for step in range(blocks):
                    weight = piece(step, part, start, stop)
                    term = jnp.dot(held[pair ^ step], weight, preferred_element_type=jnp.float32)
                    total = term if total is None else total + term
                where = slice(place * width + start, place * width + stop)
                own_ref[:, where] = total[:count]
                send_ref[:, where] = total[count:].astype(send_ref.dtype)


def relay_kernel(qkv_low, qkv_high, out_low, out_high, low_ref, high_ref):
    half = low_ref.shape[2]
    parts = qkv_low.shape[0]
    low_ref[:parts] = qkv_low[:, :, :half]
    low_ref[parts] = out_low[:half]
    high_ref[:parts] = qkv_high[:, :, half:]
    high_ref[parts] = out_high[half:]


def relayed(qkv_near, out_near):
    if len(qkv_near) != 2:
        return []
    parts, depth, _ = qkv_near[0].shape
    shape = jax.ShapeDtypeStruct((parts + 1, depth, depth), qkv_near[0].dtype)
    low, high = pl.pallas_call(
        relay_kernel,
        out_shape=(shape, shape),
        in_specs=[VMEM] * 4,
        out_specs=(VMEM, VMEM),
        compiler_params=pltpu.CompilerParams(vmem_limit_bytes=8 << 20),
        name="relay",
    )(*qkv_near, *out_near)
    return [pair_exchange(low, 2), pair_exchange(high, 1)]


def qkv_kernel(place_ref, own_in_ref, other_in_ref, *refs):
    *weight_refs, own_q, own_kv, send_q, send_kv, held = refs
    count = own_in_ref.shape[1]
    held[:, :count] = own_in_ref[...]
    held[:, count:] = other_in_ref[...]
    blocks, width = held.shape[0], own_q.shape[1]
    direct = blocks - 1 if len(weight_refs) == blocks + 1 else blocks

    def piece(step, part, start, stop):
        if step < direct:
            return weight_refs[step][part, :, start:stop]
        half = start // (width // 2)
        offset = start - half * (width // 2)
        return weight_refs[direct + half][part, :, offset : offset + stop - start]

    multiply_pieces(
        ((0,), (1, 2)), held, place_ref[0] // 2, piece, width, (own_q, own_kv), (send_q, send_kv)
    )


def project_qkv(place, own, other, pieces):
    blocks, count, depth = own.shape
    width = 2 * depth
    shapes = [jax.ShapeDtypeStruct((count, n * width), jnp.float32) for n in (1, 2)] * 2
    return pl.pallas_call(
        qkv_kernel,
        out_shape=tuple(shapes),
        in_specs=[SMEM] + [VMEM] * (2 + len(pieces)),
        out_specs=tuple([VMEM] * 4),
        scratch_shapes=[pltpu.VMEM((blocks, 2 * count, depth), jnp.bfloat16)],
        compiler_params=pltpu.CompilerParams(vmem_limit_bytes=8 << 20),
        cost_estimate=pl.CostEstimate(
            flops=12 * count * depth * blocks * width,
            bytes_accessed=6 * depth * blocks * width,
            transcendentals=0,
        ),
        name="qkv",
    )(place, own, other, *pieces)


def ffn_in_kernel(place_ref, gain_ref, *refs):
    blocks = lax.axis_size("col")
    block_refs, refs = refs[:blocks], refs[blocks:]
    *weight_refs, own_ref, send_ref, held = refs
    row, col = place_ref[0], place_ref[1]
    for step, ref in enumerate(block_refs):
        index = lax.rem(col - step + blocks, blocks)
        gain = gain_ref[pl.ds(2 * index + lax.rem(row, 2), 1), :]
        held[index] = (ref[...].astype(jnp.float32) * gain).astype(jnp.bfloat16)
    def piece(step, part, start, stop):
        return half_ref(weight_refs, step, part)[:, start:stop]

    width = weight_refs[0].shape[2]
    multiply_pieces(((0, 1),), held, row // 2, piece, width, (own_ref,), (send_ref,))


def project_ffn(place, gain, token_blocks, pieces):
    tokens_two, depth = token_blocks[0].shape
    blocks, count = len(token_blocks), tokens_two // 2
    columns = 2 * pieces[0].shape[2]
    return pl.pallas_call(
        ffn_in_kernel,
        out_shape=(
            jax.ShapeDtypeStruct((count, columns), jnp.float32),
            jax.ShapeDtypeStruct((count, columns), jnp.bfloat16),
        ),
        in_specs=[SMEM] + [VMEM] * (1 + blocks + len(pieces)),
        out_specs=(VMEM, VMEM),
        scratch_shapes=[pltpu.VMEM((blocks, tokens_two, depth), jnp.bfloat16)],
        compiler_params=pltpu.CompilerParams(vmem_limit_bytes=8 << 20),
        cost_estimate=pl.CostEstimate(
            flops=2 * tokens_two * depth * blocks * columns,
            bytes_accessed=2 * depth * blocks * columns,
            transcendentals=0,
        ),
        name="ffn_in",
    )(place, gain, *token_blocks, *pieces)


def columns_kernel(place_ref, own_in_ref, other_in_ref, *refs):
    blocks = lax.axis_size("col")
    *weight_refs, own_ref = refs[: len(refs) - blocks]
    send_refs, held = refs[len(refs) - blocks : -1], refs[-1]
    row, col = place_ref[0], place_ref[1]
    pair = row // 2
    hidden = jnp.concatenate([own_in_ref[...], other_in_ref[...]], axis=0)
    far = len(weight_refs) == blocks + 1
    direct = blocks - 1 if far else blocks
    for step in range(blocks):
        if len(weight_refs[0].shape) == 3:
            half = hidden.shape[1] // 2
            total = jnp.dot(
                hidden[:, :half],
                half_ref(weight_refs, step, 0)[...],
                preferred_element_type=jnp.float32,
            ) + jnp.dot(
                hidden[:, half:],
                half_ref(weight_refs, step, 1)[...],
                preferred_element_type=jnp.float32,
            )
        elif step < direct:
            total = jnp.dot(hidden, weight_refs[step][...], preferred_element_type=jnp.float32)
        else:
            half = hidden.shape[1] // 2
            low, high = (ref[ref.shape[0] - 1] for ref in weight_refs[direct:])
            total = jnp.dot(
                hidden[:, :half], low, preferred_element_type=jnp.float32
            ) + jnp.dot(hidden[:, half:], high, preferred_element_type=jnp.float32)
        held[lax.rem((pair ^ step) - col + blocks, blocks)] = total
    own_ref[...] = held[0]
    for step in range(1, blocks):
        send_refs[step - 1][...] = held[step].astype(jnp.bfloat16)


def columns(place, own, other, pieces, name):
    count, depth = own.shape
    width = pieces[0].shape[-1]
    blocks = lax.axis_size("col")
    return pl.pallas_call(
        columns_kernel,
        out_shape=(
            jax.ShapeDtypeStruct((2 * count, width), jnp.float32),
            *[jax.ShapeDtypeStruct((2 * count, width), jnp.bfloat16)] * (blocks - 1),
        ),
        in_specs=[SMEM] + [VMEM] * (2 + len(pieces)),
        out_specs=tuple([VMEM] * blocks),
        scratch_shapes=[pltpu.VMEM((blocks, 2 * count, width), jnp.float32)],
        compiler_params=pltpu.CompilerParams(vmem_limit_bytes=8 << 20),
        cost_estimate=pl.CostEstimate(
            flops=4 * count * depth * width * blocks,
            bytes_accessed=2 * depth * width * blocks,
            transcendentals=0,
        ),
        name=name,
    )(place, own, other, *pieces)


def summed(own, sends, residual):
    total = own + residual.astype(jnp.float32)
    for step, send in enumerate(sends, 1):
        total = total + shifted(send, step).astype(jnp.float32)
    return total.astype(jnp.bfloat16)


def gathered(block):
    return [block] + [shifted(block, step) for step in range(1, lax.axis_size("col"))]


def square_sums(blocks):
    return sum(jnp.sum(jnp.square(b.astype(jnp.float32)), axis=1) for b in blocks)


def per_device(
    tokens,
    segment_ids,
    bucket_table,
    slot_index,
    gain_attn,
    w_qkv,
    rel_bias,
    w_out,
    gain_ffn,
    w_in,
    w_down,
):
    rows, cols = lax.axis_size("row"), lax.axis_size("col")
    count, width = tokens.shape
    half = width // 2
    features = width * cols
    row, col = lax.axis_index("row"), lax.axis_index("col")
    core = row % 2
    place = jnp.stack([row, col]).astype(jnp.int32)

    qkv_near = near_pieces(w_qkv)
    token_blocks = gathered(tokens)
    kept, given = norm_tokens(place, gain_attn.reshape(cols, width), token_blocks)
    out_near = near_pieces(after(w_out, token_blocks[1]))
    token_block = jnp.concatenate(
        [
            jnp.where(core == 0, tokens[:, :half], tokens[:, half:]),
            other_core(jnp.where(core == 0, tokens[:, half:], tokens[:, :half])),
        ],
        axis=0,
    )
    bias = masked_bias(row, segment_ids, bucket_table, rel_bias, count)
    ready = lax.optimization_barrier((*qkv_near, *out_near, kept, given, bias, token_block))
    *near, kept, given, bias, token_block = ready
    received = other_core(given)
    qkv_near, out_near = near[: len(near) // 2], near[len(near) // 2 :]
    far = relayed(qkv_near, out_near)
    w_in, w_down, *_ = lax.optimization_barrier((w_in, w_down.reshape(2, -1, half), received))
    down_first = first_phase(w_down[0], w_down[1])
    in_first = first_phase(w_in[0], w_in[1])
    own_q, own_kv, send_q, send_kv = project_qkv(
        place, kept, received, [w_qkv, *qkv_near, *far]
    )
    other_kv, other_q, *down_first = lax.optimization_barrier(
        (other_core(send_kv), other_core(send_q), *down_first)
    )
    key_value = (own_kv + other_kv).astype(jnp.bfloat16)
    packets = second_phase(w_down, down_first)
    queries = (own_q + other_q).astype(jnp.bfloat16)
    forward = [(i, i + 1) for i in range(rows - 1)]
    backward = [(target, source) for source, target in forward]
    low = lax.ppermute(key_value, "row", forward)
    high = lax.ppermute(key_value, "row", backward)
    low, high, *waited = lax.optimization_barrier((low, high, *in_first, *packets))
    in_first, packets = waited[: len(in_first)], waited[len(in_first) :]
    in_pieces = [w_in, *in_first, *exchanged(second_phase(w_in, in_first))]
    context = attention(queries, low, key_value, high, bias)
    own, *sends = columns(
        place, context, other_core(context), [w_out, *out_near, *far], "attention_out"
    )
    stacked = jnp.stack([key_value[:, :width], key_value[:, width:]])
    blocks = stacked.reshape(2, slot_index.shape[1], BLOCK, width)
    kv_cache = jnp.zeros_like(blocks)
    for index in range(slot_index.shape[1]):
        kv_cache = lax.dynamic_update_slice_in_dim(
            kv_cache, blocks[:, index : index + 1], slot_index[0, index], axis=1
        )
    kv_cache = kv_cache.reshape(2, count, width)
    middle, kv_cache = lax.optimization_barrier((summed(own, sends, token_block), kv_cache))

    middle_blocks = gathered(middle)
    squares = square_sums(middle_blocks)
    squares = squares[:count] + other_core(squares[count:])
    scale = lax.rsqrt(squares / features + epsilon)[:, None]
    down_second = exchanged(after_all(packets, middle_blocks[-1]))
    own, send = project_ffn(
        place, gain_ffn.reshape(rows, -1), middle_blocks, in_pieces
    )
    scale, *down_second = lax.optimization_barrier((scale, *down_second))
    branches = (own + other_core(send).astype(jnp.float32)) * scale
    inner = branches.shape[1] // 2
    hidden = (
        jax.nn.gelu(branches[:, :inner], approximate=True) * branches[:, inner:]
    ).astype(jnp.bfloat16)
    own, *sends = columns(
        place, hidden, other_core(hidden), [w_down, *down_first, *down_second], "ffn_out"
    )
    result = summed(own, sends, middle)
    received = other_core(result[count:])
    output = jnp.where(
        core == 0,
        jnp.concatenate([result[:count], received], axis=1),
        jnp.concatenate([received, result[:count]], axis=1),
    )

    return (output, kv_cache)


def solution(mesh):
    return jax.shard_map(
        per_device,
        mesh=mesh,
        in_specs=(
            P("row", "col"),
            P(),
            P(),
            P("row", None),
            P(),
            P(None, "row", "col"),
            P(None, "col"),
            P("col", "row"),
            P(),
            P(None, "row", "col"),
            P("col", "row"),
        ),
        out_specs=(P("row", "col"), P(None, "row", "col")),
        check_vma=False,
    )
```

```python
import functools

import jax
import jax.numpy as jnp
from jax import lax
from jax.experimental import pallas as pl
from jax.experimental.pallas import tpu as pltpu
from jax.sharding import PartitionSpec as P

BLOCK = 128


epsilon = 1e-06
masked_score = -1e30
VMEM = pl.BlockSpec(memory_space=pltpu.VMEM)
SMEM = pl.BlockSpec(memory_space=pltpu.SMEM)


def bias_kernel(row_ref, seg_ref, table_ref, rel_ref, out_ref):
    heads, count, width = out_ref.shape
    rows = seg_ref.shape[0]
    row = row_ref[0]
    table = table_ref[...]
    rel = rel_ref[...]
    by_distance = jnp.zeros((heads, table.shape[1]), jnp.float32)
    for bucket in range(rel.shape[1]):
        by_distance = jnp.where(table == bucket, rel[:, bucket : bucket + 1], by_distance)
    by_distance = jnp.concatenate(
        [by_distance, jnp.zeros((heads, width - table.shape[1]), jnp.float32)], axis=1
    )

    def segment_row(index):
        clipped = jnp.clip(index, 0, rows - 1)
        found = seg_ref[pl.ds(clipped, 1), :].astype(jnp.float32)
        return jnp.where(index == clipped, found, -1.0)

    own = segment_row(row)
    query_seg = jnp.broadcast_to(own, (count, count)).T
    allowed = jnp.concatenate(
        [query_seg == segment_row(row - 1), query_seg == own, query_seg == segment_row(row + 1)],
        axis=1,
    )
    for head in range(heads):
        line = jnp.broadcast_to(by_distance[head : head + 1, :], (count, width))
        shifted = pltpu.roll(line, 1, 1, stride=1, stride_axis=0)
        out_ref[head] = jnp.where(allowed, shifted, masked_score)


def masked_bias(row, segment_ids, bucket_table, rel_bias, count):
    heads = rel_bias.shape[1]
    table = jnp.pad(bucket_table, (0, 1)).reshape(1, 2 * count)
    return pl.pallas_call(
        bias_kernel,
        out_shape=jax.ShapeDtypeStruct((heads, count, 3 * count), jnp.float32),
        in_specs=[SMEM, VMEM, VMEM, VMEM],
        out_specs=VMEM,
        compiler_params=pltpu.CompilerParams(vmem_limit_bytes=8 << 20),
        name="masked_bias",
    )(row.reshape(1), segment_ids.reshape(-1, count), table, rel_bias.T)


def attention_kernel(q_ref, low_ref, own_ref, high_ref, bias_ref, out_ref):
    heads, count, _ = bias_ref.shape
    total_width = q_ref.shape[1]
    width = total_width // heads
    sides = (low_ref, own_ref, high_ref)
    for pair in range(0, heads, 2):
        parts = []
        for head in (pair, pair + 1):
            cut = slice(head * width, (head + 1) * width)
            after_keys = slice(total_width + head * width, total_width + (head + 1) * width)
            query = q_ref[:, cut]
            scores = jnp.concatenate(
                [
                    lax.dot_general(
                        query,
                        ref[:, cut],
                        (((1,), (1,)), ((), ())),
                        preferred_element_type=jnp.float32,
                    )
                    for ref in sides
                ],
                axis=1,
            )
            scores = scores + bias_ref[head]
            top = jnp.max(scores, axis=1, keepdims=True)
            weights = jnp.exp(scores - top)
            denominator = jnp.sum(weights, axis=1, keepdims=True)
            rounded = weights.astype(jnp.bfloat16)
            total = sum(
                jnp.dot(
                    rounded[:, i * count : (i + 1) * count],
                    ref[:, after_keys],
                    preferred_element_type=jnp.float32,
                )
                for i, ref in enumerate(sides)
            )
            parts.append(total / denominator)
        out_ref[:, pair * width : (pair + 2) * width] = jnp.concatenate(parts, axis=1).astype(
            out_ref.dtype
        )


def attention(queries, low, own, high, bias):
    count, span = bias.shape[1:]
    return pl.pallas_call(
        attention_kernel,
        out_shape=jax.ShapeDtypeStruct(queries.shape, jnp.bfloat16),
        in_specs=[VMEM] * 5,
        out_specs=VMEM,
        compiler_params=pltpu.CompilerParams(vmem_limit_bytes=8 << 20),
        cost_estimate=pl.CostEstimate(
            flops=4 * queries.size * span, bytes_accessed=4 * bias.size, transcendentals=bias.size
        ),
        name="attention",
    )(queries, low, own, high, bias)


def exchange(value, axis, partner):
    count = lax.axis_size(axis)
    return lax.ppermute(value, axis, [(i, partner(i) % count) for i in range(count)])


def other_core(value):
    return exchange(value, "row", lambda i: i ^ 1)


def pair_exchange(value, step):
    return exchange(value, "row", lambda i: i ^ (2 * step))


def shifted(value, step):
    return exchange(value, "col", lambda i: i + step)


def after(value, *earlier):
    return lax.optimization_barrier((value, *earlier))[0]


def near_pieces(weight):
    pairs = lax.axis_size("row") // 2
    if pairs == 4:
        return [pair_exchange(weight, 1), pair_exchange(weight, 2)]
    return [pair_exchange(weight, step) for step in range(1, pairs)]


def after_all(values, *earlier):
    return list(lax.optimization_barrier((*values, *earlier))[: len(values)])


def first_hop(weight, *earlier):
    weight = after(weight, *earlier)
    return weight, near_pieces(weight)


def first_phase(low, high):
    pairs = lax.axis_size("row") // 2
    if pairs != 4:
        return [pair_exchange(part, step) for step in range(1, pairs) for part in (low, high)]
    return [pair_exchange(low, 1), pair_exchange(high, 2)]


def packet_kernel(own_ref, low_in, high_in, low_ref, high_ref):
    size = low_in.shape[0]
    low_ref[0], high_ref[0] = own_ref[0], own_ref[1]
    low_ref[1], high_ref[1] = low_in[...], high_in[...]


def second_phase(own, first):
    if len(first) != 2:
        return []
    shape = jax.ShapeDtypeStruct(own.shape, own.dtype)
    low, high = pl.pallas_call(
        packet_kernel,
        out_shape=(shape, shape),
        in_specs=[VMEM] * 3,
        out_specs=(VMEM, VMEM),
        compiler_params=pltpu.CompilerParams(vmem_limit_bytes=8 << 20),
        name="packet",
    )(own, *first)
    return [low, high]


def exchanged(packets):
    return [pair_exchange(packet, step) for packet, step in zip(packets[::-1], (1, 2))]


def half_ref(refs, step, part):
    own, *others = refs
    if step == 0:
        return own.at[part]
    if len(others) != 4:
        return others[2 * (step - 1) + part]
    near_low, side_high, highs, lows = others
    if step == 3:
        return (highs if part else lows).at[1]
    if part == step - 1:
        return near_low if part == 0 else side_high
    return (highs if part else lows).at[0]


def norm_kernel(place_ref, gain_ref, *refs):
    *block_refs, kept_ref, given_ref = refs
    blocks = len(block_refs)
    core, col = lax.rem(place_ref[0], 2), place_ref[1]
    wide = [ref[...].astype(jnp.float32) for ref in block_refs]
    squares = sum(jnp.sum(block * block, axis=1, keepdims=True) for block in wide)
    half = wide[0].shape[1] // 2
    scale = lax.rsqrt(squares / (2 * half * blocks) + epsilon)
    for step, block in enumerate(wide):
        index = lax.rem(col - step + blocks, blocks)
        normed = (block * scale * gain_ref[pl.ds(index, 1), :]).astype(jnp.bfloat16)
        low, high = normed[:, :half], normed[:, half:]
        kept_ref[index] = jnp.where(core == 0, low, high)
        given_ref[index] = jnp.where(core == 0, high, low)


def norm_tokens(place, gain, token_blocks):
    count, width = token_blocks[0].shape
    shape = jax.ShapeDtypeStruct((len(token_blocks), count, width // 2), jnp.bfloat16)
    return pl.pallas_call(
        norm_kernel,
        out_shape=(shape, shape),
        in_specs=[SMEM] + [VMEM] * (1 + len(token_blocks)),
        out_specs=(VMEM, VMEM),
        compiler_params=pltpu.CompilerParams(vmem_limit_bytes=8 << 20),
        name="norm_tokens",
    )(place, gain, *token_blocks)


def multiply_pieces(groups, held, pair, piece, width, own_refs, send_refs):
    blocks, tokens_two, _ = held.shape
    count = tokens_two // 2
    tile = min(256, width, held.shape[2])
    for group, own_ref, send_ref in zip(groups, own_refs, send_refs):
        for place, part in enumerate(group):
            for start in range(0, width, tile):
                stop = min(start + tile, width)
                total = None
                for step in range(blocks):
                    weight = piece(step, part, start, stop)
                    term = jnp.dot(held[pair ^ step], weight, preferred_element_type=jnp.float32)
                    total = term if total is None else total + term
                where = slice(place * width + start, place * width + stop)
                own_ref[:, where] = total[:count]
                send_ref[:, where] = total[count:].astype(send_ref.dtype)


def relay_kernel(axis, low_in, high_in, low_ref, high_ref):
    half = low_ref.shape[axis]
    low_ref[...] = low_in[:half] if axis == 0 else low_in[:, :, :half]
    high_ref[...] = high_in[half:] if axis == 0 else high_in[:, :, half:]


def relayed(near, axis, name):
    if len(near) != 2:
        return []
    dims = list(near[0].shape)
    dims[axis] //= 2
    shape = jax.ShapeDtypeStruct(tuple(dims), near[0].dtype)
    low, high = pl.pallas_call(
        functools.partial(relay_kernel, axis),
        out_shape=(shape, shape),
        in_specs=[VMEM] * 2,
        out_specs=(VMEM, VMEM),
        compiler_params=pltpu.CompilerParams(vmem_limit_bytes=8 << 20),
        name=name,
    )(*near)
    return [pair_exchange(low, 2), pair_exchange(high, 1)]


def qkv_kernel(place_ref, own_in_ref, other_in_ref, *refs):
    *weight_refs, own_q, own_kv, send_q, send_kv, held = refs
    count = own_in_ref.shape[1]
    held[:, :count] = own_in_ref[...]
    held[:, count:] = other_in_ref[...]
    blocks, width = held.shape[0], own_q.shape[1]
    direct = blocks - 1 if len(weight_refs) == blocks + 1 else blocks

    def piece(step, part, start, stop):
        if step < direct:
            return weight_refs[step][part, :, start:stop]
        half = start // (width // 2)
        offset = start - half * (width // 2)
        return weight_refs[direct + half][part, :, offset : offset + stop - start]

    multiply_pieces(
        ((0,), (1, 2)), held, place_ref[0] // 2, piece, width, (own_q, own_kv), (send_q, send_kv)
    )


def project_qkv(place, own, other, pieces):
    blocks, count, depth = own.shape
    width = 2 * depth
    shapes = [jax.ShapeDtypeStruct((count, n * width), jnp.float32) for n in (1, 2)] * 2
    return pl.pallas_call(
        qkv_kernel,
        out_shape=tuple(shapes),
        in_specs=[SMEM] + [VMEM] * (2 + len(pieces)),
        out_specs=tuple([VMEM] * 4),
        scratch_shapes=[pltpu.VMEM((blocks, 2 * count, depth), jnp.bfloat16)],
        compiler_params=pltpu.CompilerParams(vmem_limit_bytes=8 << 20),
        cost_estimate=pl.CostEstimate(
            flops=12 * count * depth * blocks * width,
            bytes_accessed=6 * depth * blocks * width,
            transcendentals=0,
        ),
        name="qkv",
    )(place, own, other, *pieces)


def ffn_in_kernel(place_ref, gain_ref, *refs):
    blocks = lax.axis_size("col")
    block_refs, refs = refs[:blocks], refs[blocks:]
    *weight_refs, own_ref, send_ref, held = refs
    row, col = place_ref[0], place_ref[1]
    for step, ref in enumerate(block_refs):
        index = lax.rem(col - step + blocks, blocks)
        gain = gain_ref[pl.ds(2 * index + lax.rem(row, 2), 1), :]
        held[index] = (ref[...].astype(jnp.float32) * gain).astype(jnp.bfloat16)
    def piece(step, part, start, stop):
        return half_ref(weight_refs, step, part)[:, start:stop]

    width = weight_refs[0].shape[2]
    multiply_pieces(((0, 1),), held, row // 2, piece, width, (own_ref,), (send_ref,))


def project_ffn(place, gain, token_blocks, pieces):
    tokens_two, depth = token_blocks[0].shape
    blocks, count = len(token_blocks), tokens_two // 2
    columns = 2 * pieces[0].shape[2]
    return pl.pallas_call(
        ffn_in_kernel,
        out_shape=(
            jax.ShapeDtypeStruct((count, columns), jnp.float32),
            jax.ShapeDtypeStruct((count, columns), jnp.bfloat16),
        ),
        in_specs=[SMEM] + [VMEM] * (1 + blocks + len(pieces)),
        out_specs=(VMEM, VMEM),
        scratch_shapes=[pltpu.VMEM((blocks, tokens_two, depth), jnp.bfloat16)],
        compiler_params=pltpu.CompilerParams(vmem_limit_bytes=8 << 20),
        cost_estimate=pl.CostEstimate(
            flops=2 * tokens_two * depth * blocks * columns,
            bytes_accessed=2 * depth * blocks * columns,
            transcendentals=0,
        ),
        name="ffn_in",
    )(place, gain, *token_blocks, *pieces)


def columns_kernel(place_ref, own_in_ref, other_in_ref, *refs):
    blocks = lax.axis_size("col")
    *weight_refs, own_ref = refs[: len(refs) - blocks]
    send_refs, held = refs[len(refs) - blocks : -1], refs[-1]
    row, col = place_ref[0], place_ref[1]
    pair = row // 2
    hidden = jnp.concatenate([own_in_ref[...], other_in_ref[...]], axis=0)
    far = len(weight_refs) == blocks + 1
    direct = blocks - 1 if far else blocks
    for step in range(blocks):
        if len(weight_refs[0].shape) == 3:
            half = hidden.shape[1] // 2
            total = jnp.dot(
                hidden[:, :half],
                half_ref(weight_refs, step, 0)[...],
                preferred_element_type=jnp.float32,
            ) + jnp.dot(
                hidden[:, half:],
                half_ref(weight_refs, step, 1)[...],
                preferred_element_type=jnp.float32,
            )
        elif step < direct:
            total = jnp.dot(hidden, weight_refs[step][...], preferred_element_type=jnp.float32)
        else:
            half = hidden.shape[1] // 2
            low, high = (ref[...] for ref in weight_refs[direct:])
            total = jnp.dot(
                hidden[:, :half], low, preferred_element_type=jnp.float32
            ) + jnp.dot(hidden[:, half:], high, preferred_element_type=jnp.float32)
        held[lax.rem((pair ^ step) - col + blocks, blocks)] = total
    own_ref[...] = held[0]
    for step in range(1, blocks):
        send_refs[step - 1][...] = held[step].astype(jnp.bfloat16)


def columns(place, own, other, pieces, name):
    count, depth = own.shape
    width = pieces[0].shape[-1]
    blocks = lax.axis_size("col")
    return pl.pallas_call(
        columns_kernel,
        out_shape=(
            jax.ShapeDtypeStruct((2 * count, width), jnp.float32),
            *[jax.ShapeDtypeStruct((2 * count, width), jnp.bfloat16)] * (blocks - 1),
        ),
        in_specs=[SMEM] + [VMEM] * (2 + len(pieces)),
        out_specs=tuple([VMEM] * blocks),
        scratch_shapes=[pltpu.VMEM((blocks, 2 * count, width), jnp.float32)],
        compiler_params=pltpu.CompilerParams(vmem_limit_bytes=8 << 20),
        cost_estimate=pl.CostEstimate(
            flops=4 * count * depth * width * blocks,
            bytes_accessed=2 * depth * width * blocks,
            transcendentals=0,
        ),
        name=name,
    )(place, own, other, *pieces)


def summed(own, sends, residual):
    total = own + residual.astype(jnp.float32)
    for step, send in enumerate(sends, 1):
        total = total + shifted(send, step).astype(jnp.float32)
    return total.astype(jnp.bfloat16)


def gathered(block):
    return [block] + [shifted(block, step) for step in range(1, lax.axis_size("col"))]


def square_sums(blocks):
    return sum(jnp.sum(jnp.square(b.astype(jnp.float32)), axis=1) for b in blocks)


def per_device(
    tokens,
    segment_ids,
    bucket_table,
    slot_index,
    gain_attn,
    w_qkv,
    rel_bias,
    w_out,
    gain_ffn,
    w_in,
    w_down,
):
    rows, cols = lax.axis_size("row"), lax.axis_size("col")
    count, width = tokens.shape
    half = width // 2
    features = width * cols
    row, col = lax.axis_index("row"), lax.axis_index("col")
    core = row % 2
    place = jnp.stack([row, col]).astype(jnp.int32)

    qkv_near = near_pieces(w_qkv)
    token_blocks = gathered(tokens)
    kept, given = norm_tokens(place, gain_attn.reshape(cols, width), token_blocks)
    out_near = near_pieces(after(w_out, token_blocks[1]))
    token_block = jnp.concatenate(
        [
            jnp.where(core == 0, tokens[:, :half], tokens[:, half:]),
            other_core(jnp.where(core == 0, tokens[:, half:], tokens[:, :half])),
        ],
        axis=0,
    )
    bias = masked_bias(row, segment_ids, bucket_table, rel_bias, count)
    *qkv_near, kept, given, token_block = lax.optimization_barrier(
        (*qkv_near, kept, given, token_block)
    )
    received = other_core(given)
    qkv_far = relayed(qkv_near, 2, "relay_qkv")
    *out_near, received, bias = lax.optimization_barrier((*out_near, received, bias))
    out_far = relayed(out_near, 0, "relay_out")
    w_in, w_down, *_ = lax.optimization_barrier((w_in, w_down.reshape(2, -1, half), received))
    down_first = first_phase(w_down[0], w_down[1])
    in_first = first_phase(w_in[0], w_in[1])
    kept, *out_far = lax.optimization_barrier((kept, *out_far))
    own_q, own_kv, send_q, send_kv = project_qkv(
        place, kept, received, [w_qkv, *qkv_near, *qkv_far]
    )
    other_kv, other_q, *down_first = lax.optimization_barrier(
        (other_core(send_kv), other_core(send_q), *down_first)
    )
    key_value = (own_kv + other_kv).astype(jnp.bfloat16)
    packets = second_phase(w_down, down_first)
    queries = (own_q + other_q).astype(jnp.bfloat16)
    forward = [(i, i + 1) for i in range(rows - 1)]
    backward = [(target, source) for source, target in forward]
    low = lax.ppermute(key_value, "row", forward)
    high = lax.ppermute(key_value, "row", backward)
    low, high, *waited = lax.optimization_barrier((low, high, *in_first, *packets))
    in_first, packets = waited[: len(in_first)], waited[len(in_first) :]
    in_pieces = [w_in, *in_first, *exchanged(second_phase(w_in, in_first))]
    context = attention(queries, low, key_value, high, bias)
    own, *sends = columns(
        place, context, other_core(context), [w_out, *out_near, *out_far], "attention_out"
    )
    stacked = jnp.stack([key_value[:, :width], key_value[:, width:]])
    blocks = stacked.reshape(2, slot_index.shape[1], BLOCK, width)
    kv_cache = jnp.zeros_like(blocks)
    for index in range(slot_index.shape[1]):
        kv_cache = lax.dynamic_update_slice_in_dim(
            kv_cache, blocks[:, index : index + 1], slot_index[0, index], axis=1
        )
    kv_cache = kv_cache.reshape(2, count, width)
    middle, kv_cache = lax.optimization_barrier((summed(own, sends, token_block), kv_cache))

    middle_blocks = gathered(middle)
    squares = square_sums(middle_blocks)
    squares = squares[:count] + other_core(squares[count:])
    scale = lax.rsqrt(squares / features + epsilon)[:, None]
    down_second = exchanged(after_all(packets, middle_blocks[-1]))
    own, send = project_ffn(
        place, gain_ffn.reshape(rows, -1), middle_blocks, in_pieces
    )
    scale, *down_second = lax.optimization_barrier((scale, *down_second))
    branches = (own + other_core(send).astype(jnp.float32)) * scale
    inner = branches.shape[1] // 2
    hidden = (
        jax.nn.gelu(branches[:, :inner], approximate=True) * branches[:, inner:]
    ).astype(jnp.bfloat16)
    own, *sends = columns(
        place, hidden, other_core(hidden), [w_down, *down_first, *down_second], "ffn_out"
    )
    result = summed(own, sends, middle)
    received = other_core(result[count:])
    output = jnp.where(
        core == 0,
        jnp.concatenate([result[:count], received], axis=1),
        jnp.concatenate([received, result[:count]], axis=1),
    )

    return (output, kv_cache)


def solution(mesh):
    return jax.shard_map(
        per_device,
        mesh=mesh,
        in_specs=(
            P("row", "col"),
            P(),
            P(),
            P("row", None),
            P(),
            P(None, "row", "col"),
            P(None, "col"),
            P("col", "row"),
            P(),
            P(None, "row", "col"),
            P("col", "row"),
        ),
        out_specs=(P("row", "col"), P(None, "row", "col")),
        check_vma=False,
    )
```

```python
import functools

import jax
import jax.numpy as jnp
from jax import lax
from jax.experimental import pallas as pl
from jax.experimental.pallas import tpu as pltpu
from jax.sharding import PartitionSpec as P

BLOCK = 128


epsilon = 1e-06
masked_score = -1e30
VMEM = pl.BlockSpec(memory_space=pltpu.VMEM)
SMEM = pl.BlockSpec(memory_space=pltpu.SMEM)


def bias_kernel(row_ref, seg_ref, table_ref, rel_ref, out_ref):
    heads, count, width = out_ref.shape
    rows = seg_ref.shape[0]
    row = row_ref[0]
    table = table_ref[...]
    rel = rel_ref[...]
    by_distance = jnp.zeros((heads, table.shape[1]), jnp.float32)
    for bucket in range(rel.shape[1]):
        by_distance = jnp.where(table == bucket, rel[:, bucket : bucket + 1], by_distance)
    by_distance = jnp.concatenate(
        [by_distance, jnp.zeros((heads, width - table.shape[1]), jnp.float32)], axis=1
    )

    def segment_row(index):
        clipped = jnp.clip(index, 0, rows - 1)
        found = seg_ref[pl.ds(clipped, 1), :].astype(jnp.float32)
        return jnp.where(index == clipped, found, -1.0)

    own = segment_row(row)
    query_seg = jnp.broadcast_to(own, (count, count)).T
    allowed = jnp.concatenate(
        [query_seg == segment_row(row - 1), query_seg == own, query_seg == segment_row(row + 1)],
        axis=1,
    )
    for head in range(heads):
        line = jnp.broadcast_to(by_distance[head : head + 1, :], (count, width))
        shifted = pltpu.roll(line, 1, 1, stride=1, stride_axis=0)
        out_ref[head] = jnp.where(allowed, shifted, masked_score)


def masked_bias(row, segment_ids, bucket_table, rel_bias, count):
    heads = rel_bias.shape[1]
    table = jnp.pad(bucket_table, (0, 1)).reshape(1, 2 * count)
    return pl.pallas_call(
        bias_kernel,
        out_shape=jax.ShapeDtypeStruct((heads, count, 3 * count), jnp.float32),
        in_specs=[SMEM, VMEM, VMEM, VMEM],
        out_specs=VMEM,
        compiler_params=pltpu.CompilerParams(vmem_limit_bytes=8 << 20),
        name="masked_bias",
    )(row.reshape(1), segment_ids.reshape(-1, count), table, rel_bias.T)


def attention_kernel(q_ref, low_ref, own_ref, high_ref, bias_ref, out_ref):
    heads, count, _ = bias_ref.shape
    total_width = q_ref.shape[1]
    width = total_width // heads
    sides = (low_ref, own_ref, high_ref)
    for pair in range(0, heads, 2):
        parts = []
        for head in (pair, pair + 1):
            cut = slice(head * width, (head + 1) * width)
            after_keys = slice(total_width + head * width, total_width + (head + 1) * width)
            query = q_ref[:, cut]
            scores = jnp.concatenate(
                [
                    lax.dot_general(
                        query,
                        ref[:, cut],
                        (((1,), (1,)), ((), ())),
                        preferred_element_type=jnp.float32,
                    )
                    for ref in sides
                ],
                axis=1,
            )
            scores = scores + bias_ref[head]
            top = jnp.max(scores, axis=1, keepdims=True)
            weights = jnp.exp(scores - top)
            denominator = jnp.sum(weights, axis=1, keepdims=True)
            rounded = weights.astype(jnp.bfloat16)
            total = sum(
                jnp.dot(
                    rounded[:, i * count : (i + 1) * count],
                    ref[:, after_keys],
                    preferred_element_type=jnp.float32,
                )
                for i, ref in enumerate(sides)
            )
            parts.append(total / denominator)
        out_ref[:, pair * width : (pair + 2) * width] = jnp.concatenate(parts, axis=1).astype(
            out_ref.dtype
        )


def attention(queries, low, own, high, bias):
    count, span = bias.shape[1:]
    return pl.pallas_call(
        attention_kernel,
        out_shape=jax.ShapeDtypeStruct(queries.shape, jnp.bfloat16),
        in_specs=[VMEM] * 5,
        out_specs=VMEM,
        compiler_params=pltpu.CompilerParams(vmem_limit_bytes=8 << 20),
        cost_estimate=pl.CostEstimate(
            flops=4 * queries.size * span, bytes_accessed=4 * bias.size, transcendentals=bias.size
        ),
        name="attention",
    )(queries, low, own, high, bias)


def exchange(value, axis, partner):
    count = lax.axis_size(axis)
    return lax.ppermute(value, axis, [(i, partner(i) % count) for i in range(count)])


def other_core(value):
    return exchange(value, "row", lambda i: i ^ 1)


def pair_exchange(value, step):
    return exchange(value, "row", lambda i: i ^ (2 * step))


def shifted(value, step):
    return exchange(value, "col", lambda i: i + step)


def after(value, *earlier):
    return lax.optimization_barrier((value, *earlier))[0]


def near_pieces(weight):
    pairs = lax.axis_size("row") // 2
    if pairs == 4:
        return [pair_exchange(weight, 1), pair_exchange(weight, 2)]
    return [pair_exchange(weight, step) for step in range(1, pairs)]


def after_all(values, *earlier):
    return list(lax.optimization_barrier((*values, *earlier))[: len(values)])


def first_hop(weight, *earlier):
    weight = after(weight, *earlier)
    return weight, near_pieces(weight)


def first_phase(low, high):
    pairs = lax.axis_size("row") // 2
    if pairs != 4:
        return [pair_exchange(part, step) for step in range(1, pairs) for part in (low, high)]
    return [pair_exchange(low, 1), pair_exchange(high, 2)]


def packet_kernel(own_ref, low_in, high_in, low_ref, high_ref):
    cut = low_in.shape[0]
    stacked = len(own_ref.shape) == 3
    low_ref[0] = own_ref[0] if stacked else own_ref[:cut]
    high_ref[0] = own_ref[1] if stacked else own_ref[cut:]
    low_ref[1], high_ref[1] = low_in[...], high_in[...]


def second_phase(own, first):
    if len(first) != 2:
        return []
    low, high = pl.pallas_call(
        packet_kernel,
        out_shape=tuple(jax.ShapeDtypeStruct((2, *part.shape), part.dtype) for part in first),
        in_specs=[VMEM] * 3,
        out_specs=(VMEM, VMEM),
        compiler_params=pltpu.CompilerParams(vmem_limit_bytes=8 << 20),
        name="packet",
    )(own, *first)
    return [low, high]


def exchanged(packets):
    return [pair_exchange(packet, step) for packet, step in zip(packets[::-1], (1, 2))]


def half_ref(refs, step, part):
    own, *others = refs
    if step == 0:
        return own.at[part]
    if len(others) != 4:
        return others[2 * (step - 1) + part]
    near_low, side_high, highs, lows = others
    if step == 3:
        return (highs if part else lows).at[1]
    if part == step - 1:
        return near_low if part == 0 else side_high
    return (highs if part else lows).at[0]


def norm_kernel(place_ref, gain_ref, *refs):
    *block_refs, kept_ref, given_ref = refs
    blocks = len(block_refs)
    core, col = lax.rem(place_ref[0], 2), place_ref[1]
    wide = [ref[...].astype(jnp.float32) for ref in block_refs]
    squares = sum(jnp.sum(block * block, axis=1, keepdims=True) for block in wide)
    half = wide[0].shape[1] // 2
    scale = lax.rsqrt(squares / (2 * half * blocks) + epsilon)
    for step, block in enumerate(wide):
        index = lax.rem(col - step + blocks, blocks)
        normed = (block * scale * gain_ref[pl.ds(index, 1), :]).astype(jnp.bfloat16)
        low, high = normed[:, :half], normed[:, half:]
        kept_ref[index] = jnp.where(core == 0, low, high)
        given_ref[index] = jnp.where(core == 0, high, low)


def norm_tokens(place, gain, token_blocks):
    count, width = token_blocks[0].shape
    shape = jax.ShapeDtypeStruct((len(token_blocks), count, width // 2), jnp.bfloat16)
    return pl.pallas_call(
        norm_kernel,
        out_shape=(shape, shape),
        in_specs=[SMEM] + [VMEM] * (1 + len(token_blocks)),
        out_specs=(VMEM, VMEM),
        compiler_params=pltpu.CompilerParams(vmem_limit_bytes=8 << 20),
        name="norm_tokens",
    )(place, gain, *token_blocks)


def multiply_pieces(groups, held, pair, piece, width, own_refs, send_refs):
    blocks, tokens_two, _ = held.shape
    count = tokens_two // 2
    tile = min(256, width, held.shape[2])
    for group, own_ref, send_ref in zip(groups, own_refs, send_refs):
        for place, part in enumerate(group):
            for start in range(0, width, tile):
                stop = min(start + tile, width)
                total = None
                for step in range(blocks):
                    weight = piece(step, part, start, stop)
                    term = jnp.dot(held[pair ^ step], weight, preferred_element_type=jnp.float32)
                    total = term if total is None else total + term
                where = slice(place * width + start, place * width + stop)
                own_ref[:, where] = total[:count]
                send_ref[:, where] = total[count:].astype(send_ref.dtype)


def relay_kernel(axis, low_in, high_in, low_ref, high_ref):
    half = low_ref.shape[axis]
    low_ref[...] = low_in[:half] if axis == 0 else low_in[:, :, :half]
    high_ref[...] = high_in[half:] if axis == 0 else high_in[:, :, half:]


def relayed(near, axis, name):
    if len(near) != 2:
        return []
    dims = list(near[0].shape)
    dims[axis] //= 2
    shape = jax.ShapeDtypeStruct(tuple(dims), near[0].dtype)
    low, high = pl.pallas_call(
        functools.partial(relay_kernel, axis),
        out_shape=(shape, shape),
        in_specs=[VMEM] * 2,
        out_specs=(VMEM, VMEM),
        compiler_params=pltpu.CompilerParams(vmem_limit_bytes=8 << 20),
        name=name,
    )(*near)
    return [pair_exchange(low, 2), pair_exchange(high, 1)]


def qkv_kernel(place_ref, own_in_ref, other_in_ref, *refs):
    *weight_refs, own_q, own_kv, send_q, send_kv, held = refs
    count = own_in_ref.shape[1]
    held[:, :count] = own_in_ref[...]
    held[:, count:] = other_in_ref[...]
    blocks, width = held.shape[0], own_q.shape[1]
    direct = blocks - 1 if len(weight_refs) == blocks + 1 else blocks

    def piece(step, part, start, stop):
        if step < direct:
            return weight_refs[step][part, :, start:stop]
        half = start // (width // 2)
        offset = start - half * (width // 2)
        return weight_refs[direct + half][part, :, offset : offset + stop - start]

    multiply_pieces(
        ((0,), (1, 2)), held, place_ref[0] // 2, piece, width, (own_q, own_kv), (send_q, send_kv)
    )


def project_qkv(place, own, other, pieces):
    blocks, count, depth = own.shape
    width = 2 * depth
    shapes = [jax.ShapeDtypeStruct((count, n * width), jnp.float32) for n in (1, 2)] * 2
    return pl.pallas_call(
        qkv_kernel,
        out_shape=tuple(shapes),
        in_specs=[SMEM] + [VMEM] * (2 + len(pieces)),
        out_specs=tuple([VMEM] * 4),
        scratch_shapes=[pltpu.VMEM((blocks, 2 * count, depth), jnp.bfloat16)],
        compiler_params=pltpu.CompilerParams(vmem_limit_bytes=8 << 20),
        cost_estimate=pl.CostEstimate(
            flops=12 * count * depth * blocks * width,
            bytes_accessed=6 * depth * blocks * width,
            transcendentals=0,
        ),
        name="qkv",
    )(place, own, other, *pieces)


def ffn_in_kernel(place_ref, gain_ref, *refs):
    blocks = lax.axis_size("col")
    block_refs, refs = refs[:blocks], refs[blocks:]
    *weight_refs, own_ref, send_ref, held = refs
    row, col = place_ref[0], place_ref[1]
    for step, ref in enumerate(block_refs):
        index = lax.rem(col - step + blocks, blocks)
        gain = gain_ref[pl.ds(2 * index + lax.rem(row, 2), 1), :]
        held[index] = (ref[...].astype(jnp.float32) * gain).astype(jnp.bfloat16)
    def piece(step, part, start, stop):
        return half_ref(weight_refs, step, part)[:, start:stop]

    width = weight_refs[0].shape[2]
    multiply_pieces(((0, 1),), held, row // 2, piece, width, (own_ref,), (send_ref,))


def project_ffn(place, gain, token_blocks, pieces):
    tokens_two, depth = token_blocks[0].shape
    blocks, count = len(token_blocks), tokens_two // 2
    columns = 2 * pieces[0].shape[2]
    return pl.pallas_call(
        ffn_in_kernel,
        out_shape=(
            jax.ShapeDtypeStruct((count, columns), jnp.float32),
            jax.ShapeDtypeStruct((count, columns), jnp.bfloat16),
        ),
        in_specs=[SMEM] + [VMEM] * (1 + blocks + len(pieces)),
        out_specs=(VMEM, VMEM),
        scratch_shapes=[pltpu.VMEM((blocks, tokens_two, depth), jnp.bfloat16)],
        compiler_params=pltpu.CompilerParams(vmem_limit_bytes=8 << 20),
        cost_estimate=pl.CostEstimate(
            flops=2 * tokens_two * depth * blocks * columns,
            bytes_accessed=2 * depth * blocks * columns,
            transcendentals=0,
        ),
        name="ffn_in",
    )(place, gain, *token_blocks, *pieces)


def columns_kernel(cut, place_ref, own_in_ref, other_in_ref, *refs):
    blocks = lax.axis_size("col")
    *weight_refs, own_ref = refs[: len(refs) - blocks]
    send_refs, held = refs[len(refs) - blocks : -1], refs[-1]
    row, col = place_ref[0], place_ref[1]
    pair = row // 2
    hidden = jnp.concatenate([own_in_ref[...], other_in_ref[...]], axis=0)
    far = len(weight_refs) == blocks + 1
    direct = blocks - 1 if far else blocks
    for step in range(blocks):
        if cut:
            low, high = (
                weight_refs[0][:cut] if step == 0 else half_ref(weight_refs, step, 0)[...],
                weight_refs[0][cut:] if step == 0 else half_ref(weight_refs, step, 1)[...],
            )
            total = jnp.dot(
                hidden[:, :cut], low, preferred_element_type=jnp.float32
            ) + jnp.dot(hidden[:, cut:], high, preferred_element_type=jnp.float32)
        elif step < direct:
            total = jnp.dot(hidden, weight_refs[step][...], preferred_element_type=jnp.float32)
        else:
            half = hidden.shape[1] // 2
            low, high = (ref[...] for ref in weight_refs[direct:])
            total = jnp.dot(
                hidden[:, :half], low, preferred_element_type=jnp.float32
            ) + jnp.dot(hidden[:, half:], high, preferred_element_type=jnp.float32)
        held[lax.rem((pair ^ step) - col + blocks, blocks)] = total
    own_ref[...] = held[0]
    for step in range(1, blocks):
        send_refs[step - 1][...] = held[step].astype(jnp.bfloat16)


def columns(place, own, other, pieces, name, cut=0):
    count, depth = own.shape
    width = pieces[0].shape[-1]
    blocks = lax.axis_size("col")
    return pl.pallas_call(
        functools.partial(columns_kernel, cut),
        out_shape=(
            jax.ShapeDtypeStruct((2 * count, width), jnp.float32),
            *[jax.ShapeDtypeStruct((2 * count, width), jnp.bfloat16)] * (blocks - 1),
        ),
        in_specs=[SMEM] + [VMEM] * (2 + len(pieces)),
        out_specs=tuple([VMEM] * blocks),
        scratch_shapes=[pltpu.VMEM((blocks, 2 * count, width), jnp.float32)],
        compiler_params=pltpu.CompilerParams(vmem_limit_bytes=8 << 20),
        cost_estimate=pl.CostEstimate(
            flops=4 * count * depth * width * blocks,
            bytes_accessed=2 * depth * width * blocks,
            transcendentals=0,
        ),
        name=name,
    )(place, own, other, *pieces)


def summed(own, sends, residual):
    total = own + residual.astype(jnp.float32)
    for step, send in enumerate(sends, 1):
        total = total + shifted(send, step).astype(jnp.float32)
    return total.astype(jnp.bfloat16)


def gathered(block):
    return [block] + [shifted(block, step) for step in range(1, lax.axis_size("col"))]


def square_sums(blocks):
    return sum(jnp.sum(jnp.square(b.astype(jnp.float32)), axis=1) for b in blocks)


def per_device(
    tokens,
    segment_ids,
    bucket_table,
    slot_index,
    gain_attn,
    w_qkv,
    rel_bias,
    w_out,
    gain_ffn,
    w_in,
    w_down,
):
    rows, cols = lax.axis_size("row"), lax.axis_size("col")
    count, width = tokens.shape
    half = width // 2
    features = width * cols
    row, col = lax.axis_index("row"), lax.axis_index("col")
    core = row % 2
    place = jnp.stack([row, col]).astype(jnp.int32)

    qkv_near = near_pieces(w_qkv)
    token_blocks = gathered(tokens)
    kept, given = norm_tokens(place, gain_attn.reshape(cols, width), token_blocks)
    out_near = near_pieces(after(w_out, token_blocks[1]))
    token_block = jnp.concatenate(
        [
            jnp.where(core == 0, tokens[:, :half], tokens[:, half:]),
            other_core(jnp.where(core == 0, tokens[:, half:], tokens[:, :half])),
        ],
        axis=0,
    )
    bias = masked_bias(row, segment_ids, bucket_table, rel_bias, count)
    *qkv_near, kept, given, token_block = lax.optimization_barrier(
        (*qkv_near, kept, given, token_block)
    )
    received = other_core(given)
    qkv_far = relayed(qkv_near, 2, "relay_qkv")
    *out_near, received, bias = lax.optimization_barrier((*out_near, received, bias))
    out_far = relayed(out_near, 0, "relay_out")
    w_in, w_down, *_ = lax.optimization_barrier((w_in, w_down, received))
    cut = w_down.shape[0] * 9 // 20 // 16 * 16
    down_first = first_phase(w_down[:cut], w_down[cut:])
    in_first = first_phase(w_in[0], w_in[1])
    kept, *out_far = lax.optimization_barrier((kept, *out_far))
    own_q, own_kv, send_q, send_kv = project_qkv(
        place, kept, received, [w_qkv, *qkv_near, *qkv_far]
    )
    other_kv, other_q, *down_first = lax.optimization_barrier(
        (other_core(send_kv), other_core(send_q), *down_first)
    )
    key_value = (own_kv + other_kv).astype(jnp.bfloat16)
    packets = second_phase(w_down, down_first)
    queries = (own_q + other_q).astype(jnp.bfloat16)
    forward = [(i, i + 1) for i in range(rows - 1)]
    backward = [(target, source) for source, target in forward]
    low = lax.ppermute(key_value, "row", forward)
    high = lax.ppermute(key_value, "row", backward)
    low, high, *waited = lax.optimization_barrier((low, high, *in_first, *packets))
    in_first, packets = waited[: len(in_first)], waited[len(in_first) :]
    in_pieces = [w_in, *in_first, *exchanged(second_phase(w_in, in_first))]
    context = attention(queries, low, key_value, high, bias)
    own, *sends = columns(
        place, context, other_core(context), [w_out, *out_near, *out_far], "attention_out"
    )
    stacked = jnp.stack([key_value[:, :width], key_value[:, width:]])
    blocks = stacked.reshape(2, slot_index.shape[1], BLOCK, width)
    kv_cache = jnp.zeros_like(blocks)
    for index in range(slot_index.shape[1]):
        kv_cache = lax.dynamic_update_slice_in_dim(
            kv_cache, blocks[:, index : index + 1], slot_index[0, index], axis=1
        )
    kv_cache = kv_cache.reshape(2, count, width)
    middle, kv_cache = lax.optimization_barrier((summed(own, sends, token_block), kv_cache))

    middle_blocks = gathered(middle)
    squares = square_sums(middle_blocks)
    squares = squares[:count] + other_core(squares[count:])
    scale = lax.rsqrt(squares / features + epsilon)[:, None]
    down_second = exchanged(after_all(packets, middle_blocks[-1]))
    own, send = project_ffn(
        place, gain_ffn.reshape(rows, -1), middle_blocks, in_pieces
    )
    scale, *down_second = lax.optimization_barrier((scale, *down_second))
    branches = (own + other_core(send).astype(jnp.float32)) * scale
    inner = branches.shape[1] // 2
    hidden = (
        jax.nn.gelu(branches[:, :inner], approximate=True) * branches[:, inner:]
    ).astype(jnp.bfloat16)
    own, *sends = columns(
        place, hidden, other_core(hidden), [w_down, *down_first, *down_second], "ffn_out", cut
    )
    result = summed(own, sends, middle)
    received = other_core(result[count:])
    output = jnp.where(
        core == 0,
        jnp.concatenate([result[:count], received], axis=1),
        jnp.concatenate([received, result[:count]], axis=1),
    )

    return (output, kv_cache)


def solution(mesh):
    return jax.shard_map(
        per_device,
        mesh=mesh,
        in_specs=(
            P("row", "col"),
            P(),
            P(),
            P("row", None),
            P(),
            P(None, "row", "col"),
            P(None, "col"),
            P("col", "row"),
            P(),
            P(None, "row", "col"),
            P("col", "row"),
        ),
        out_specs=(P("row", "col"), P(None, "row", "col")),
        check_vma=False,
    )
```

```python
import functools

import jax
import jax.numpy as jnp
from jax import lax
from jax.experimental import pallas as pl
from jax.experimental.pallas import tpu as pltpu
from jax.sharding import PartitionSpec as P

BLOCK = 128


epsilon = 1e-06
masked_score = -1e30
VMEM = pl.BlockSpec(memory_space=pltpu.VMEM)
SMEM = pl.BlockSpec(memory_space=pltpu.SMEM)


def bias_kernel(row_ref, seg_ref, table_ref, rel_ref, out_ref):
    heads, count, width = out_ref.shape
    rows = seg_ref.shape[0]
    row = row_ref[0]
    table = table_ref[...]
    rel = rel_ref[...]
    by_distance = jnp.zeros((heads, table.shape[1]), jnp.float32)
    for bucket in range(rel.shape[1]):
        by_distance = jnp.where(table == bucket, rel[:, bucket : bucket + 1], by_distance)
    by_distance = jnp.concatenate(
        [by_distance, jnp.zeros((heads, width - table.shape[1]), jnp.float32)], axis=1
    )

    def segment_row(index):
        clipped = jnp.clip(index, 0, rows - 1)
        found = seg_ref[pl.ds(clipped, 1), :].astype(jnp.float32)
        return jnp.where(index == clipped, found, -1.0)

    own = segment_row(row)
    query_seg = jnp.broadcast_to(own, (count, count)).T
    allowed = jnp.concatenate(
        [query_seg == segment_row(row - 1), query_seg == own, query_seg == segment_row(row + 1)],
        axis=1,
    )
    for head in range(heads):
        line = jnp.broadcast_to(by_distance[head : head + 1, :], (count, width))
        shifted = pltpu.roll(line, 1, 1, stride=1, stride_axis=0)
        out_ref[head] = jnp.where(allowed, shifted, masked_score)


def masked_bias(row, segment_ids, bucket_table, rel_bias, count):
    heads = rel_bias.shape[1]
    table = jnp.pad(bucket_table, (0, 1)).reshape(1, 2 * count)
    return pl.pallas_call(
        bias_kernel,
        out_shape=jax.ShapeDtypeStruct((heads, count, 3 * count), jnp.float32),
        in_specs=[SMEM, VMEM, VMEM, VMEM],
        out_specs=VMEM,
        compiler_params=pltpu.CompilerParams(vmem_limit_bytes=8 << 20),
        name="masked_bias",
    )(row.reshape(1), segment_ids.reshape(-1, count), table, rel_bias.T)


def attention_kernel(q_ref, low_ref, own_ref, high_ref, bias_ref, out_ref):
    heads, count, _ = bias_ref.shape
    total_width = q_ref.shape[1]
    width = total_width // heads
    sides = (low_ref, own_ref, high_ref)
    for pair in range(0, heads, 2):
        parts = []
        for head in (pair, pair + 1):
            cut = slice(head * width, (head + 1) * width)
            after_keys = slice(total_width + head * width, total_width + (head + 1) * width)
            query = q_ref[:, cut]
            scores = jnp.concatenate(
                [
                    lax.dot_general(
                        query,
                        ref[:, cut],
                        (((1,), (1,)), ((), ())),
                        preferred_element_type=jnp.float32,
                    )
                    for ref in sides
                ],
                axis=1,
            )
            scores = scores + bias_ref[head]
            top = jnp.max(scores, axis=1, keepdims=True)
            weights = jnp.exp(scores - top)
            denominator = jnp.sum(weights, axis=1, keepdims=True)
            rounded = weights.astype(jnp.bfloat16)
            total = sum(
                jnp.dot(
                    rounded[:, i * count : (i + 1) * count],
                    ref[:, after_keys],
                    preferred_element_type=jnp.float32,
                )
                for i, ref in enumerate(sides)
            )
            parts.append(total / denominator)
        out_ref[:, pair * width : (pair + 2) * width] = jnp.concatenate(parts, axis=1).astype(
            out_ref.dtype
        )


def attention(queries, low, own, high, bias):
    count, span = bias.shape[1:]
    return pl.pallas_call(
        attention_kernel,
        out_shape=jax.ShapeDtypeStruct(queries.shape, jnp.bfloat16),
        in_specs=[VMEM] * 5,
        out_specs=VMEM,
        compiler_params=pltpu.CompilerParams(vmem_limit_bytes=8 << 20),
        cost_estimate=pl.CostEstimate(
            flops=4 * queries.size * span, bytes_accessed=4 * bias.size, transcendentals=bias.size
        ),
        name="attention",
    )(queries, low, own, high, bias)


def exchange(value, axis, partner):
    count = lax.axis_size(axis)
    return lax.ppermute(value, axis, [(i, partner(i) % count) for i in range(count)])


def other_core(value):
    return exchange(value, "row", lambda i: i ^ 1)


def pair_exchange(value, step):
    return exchange(value, "row", lambda i: i ^ (2 * step))


def shifted(value, step):
    return exchange(value, "col", lambda i: i + step)


def after(value, *earlier):
    return lax.optimization_barrier((value, *earlier))[0]


def near_pieces(weight):
    pairs = lax.axis_size("row") // 2
    if pairs == 4:
        return [pair_exchange(weight, 1), pair_exchange(weight, 2)]
    return [pair_exchange(weight, step) for step in range(1, pairs)]


def after_all(values, *earlier):
    return list(lax.optimization_barrier((*values, *earlier))[: len(values)])


def first_hop(weight, *earlier):
    weight = after(weight, *earlier)
    return weight, near_pieces(weight)


def first_phase(low, high):
    pairs = lax.axis_size("row") // 2
    if pairs != 4:
        return [pair_exchange(part, step) for step in range(1, pairs) for part in (low, high)]
    return [pair_exchange(low, 1), pair_exchange(high, 2)]


def packet_kernel(own_ref, low_in, high_in, low_ref, high_ref):
    cut = low_in.shape[0]
    stacked = len(own_ref.shape) == 3
    low_ref[0] = own_ref[0] if stacked else own_ref[:cut]
    high_ref[0] = own_ref[1] if stacked else own_ref[cut:]
    low_ref[1], high_ref[1] = low_in[...], high_in[...]


def second_phase(own, first):
    if len(first) != 2:
        return []
    low, high = pl.pallas_call(
        packet_kernel,
        out_shape=tuple(jax.ShapeDtypeStruct((2, *part.shape), part.dtype) for part in first),
        in_specs=[VMEM] * 3,
        out_specs=(VMEM, VMEM),
        compiler_params=pltpu.CompilerParams(vmem_limit_bytes=8 << 20),
        name="packet",
    )(own, *first)
    return [low, high]


def exchanged(packets):
    return [pair_exchange(packet, step) for packet, step in zip(packets[::-1], (1, 2))]


def half_ref(refs, step, part):
    own, *others = refs
    if step == 0:
        return own.at[part]
    if len(others) != 4:
        return others[2 * (step - 1) + part]
    near_low, side_high, highs, lows = others
    if step == 3:
        return (highs if part else lows).at[1]
    if part == step - 1:
        return near_low if part == 0 else side_high
    return (highs if part else lows).at[0]


def norm_kernel(place_ref, gain_ref, *refs):
    *block_refs, kept_ref, given_ref = refs
    blocks = len(block_refs)
    core, col = lax.rem(place_ref[0], 2), place_ref[1]
    wide = [ref[...].astype(jnp.float32) for ref in block_refs]
    squares = sum(jnp.sum(block * block, axis=1, keepdims=True) for block in wide)
    half = wide[0].shape[1] // 2
    scale = lax.rsqrt(squares / (2 * half * blocks) + epsilon)
    for step, block in enumerate(wide):
        index = lax.rem(col - step + blocks, blocks)
        normed = (block * scale * gain_ref[pl.ds(index, 1), :]).astype(jnp.bfloat16)
        low, high = normed[:, :half], normed[:, half:]
        kept_ref[index] = jnp.where(core == 0, low, high)
        given_ref[index] = jnp.where(core == 0, high, low)


def norm_tokens(place, gain, token_blocks):
    count, width = token_blocks[0].shape
    shape = jax.ShapeDtypeStruct((len(token_blocks), count, width // 2), jnp.bfloat16)
    return pl.pallas_call(
        norm_kernel,
        out_shape=(shape, shape),
        in_specs=[SMEM] + [VMEM] * (1 + len(token_blocks)),
        out_specs=(VMEM, VMEM),
        compiler_params=pltpu.CompilerParams(vmem_limit_bytes=8 << 20),
        name="norm_tokens",
    )(place, gain, *token_blocks)


def multiply_pieces(groups, held, pair, piece, width, own_refs, send_refs):
    blocks, tokens_two, _ = held.shape
    count = tokens_two // 2
    tile = min(256, width, held.shape[2])
    for group, own_ref, send_ref in zip(groups, own_refs, send_refs):
        for place, part in enumerate(group):
            for start in range(0, width, tile):
                stop = min(start + tile, width)
                total = None
                for step in range(blocks):
                    weight = piece(step, part, start, stop)
                    term = jnp.dot(held[pair ^ step], weight, preferred_element_type=jnp.float32)
                    total = term if total is None else total + term
                where = slice(place * width + start, place * width + stop)
                own_ref[:, where] = total[:count]
                send_ref[:, where] = total[count:].astype(send_ref.dtype)


def relay_kernel(axis, low_in, high_in, low_ref, high_ref):
    half = low_ref.shape[axis]
    low_ref[...] = low_in[:half] if axis == 0 else low_in[:, :, :half]
    high_ref[...] = high_in[half:] if axis == 0 else high_in[:, :, half:]


def relayed(near, axis, name):
    if len(near) != 2:
        return []
    dims = list(near[0].shape)
    dims[axis] //= 2
    shape = jax.ShapeDtypeStruct(tuple(dims), near[0].dtype)
    low, high = pl.pallas_call(
        functools.partial(relay_kernel, axis),
        out_shape=(shape, shape),
        in_specs=[VMEM] * 2,
        out_specs=(VMEM, VMEM),
        compiler_params=pltpu.CompilerParams(vmem_limit_bytes=8 << 20),
        name=name,
    )(*near)
    return [pair_exchange(low, 2), pair_exchange(high, 1)]


def qkv_kernel(place_ref, own_in_ref, other_in_ref, *refs):
    *weight_refs, own_q, own_kv, send_q, send_kv, held = refs
    count = own_in_ref.shape[1]
    held[:, :count] = own_in_ref[...]
    held[:, count:] = other_in_ref[...]
    blocks, width = held.shape[0], own_q.shape[1]
    direct = blocks - 1 if len(weight_refs) == blocks + 1 else blocks

    def piece(step, part, start, stop):
        if step < direct:
            return weight_refs[step][part, :, start:stop]
        half = start // (width // 2)
        offset = start - half * (width // 2)
        return weight_refs[direct + half][part, :, offset : offset + stop - start]

    multiply_pieces(
        ((0,), (1, 2)), held, place_ref[0] // 2, piece, width, (own_q, own_kv), (send_q, send_kv)
    )


def project_qkv(place, own, other, pieces):
    blocks, count, depth = own.shape
    width = 2 * depth
    shapes = [jax.ShapeDtypeStruct((count, n * width), jnp.float32) for n in (1, 2)] * 2
    return pl.pallas_call(
        qkv_kernel,
        out_shape=tuple(shapes),
        in_specs=[SMEM] + [VMEM] * (2 + len(pieces)),
        out_specs=tuple([VMEM] * 4),
        scratch_shapes=[pltpu.VMEM((blocks, 2 * count, depth), jnp.bfloat16)],
        compiler_params=pltpu.CompilerParams(vmem_limit_bytes=8 << 20),
        cost_estimate=pl.CostEstimate(
            flops=12 * count * depth * blocks * width,
            bytes_accessed=6 * depth * blocks * width,
            transcendentals=0,
        ),
        name="qkv",
    )(place, own, other, *pieces)


def ffn_in_kernel(place_ref, gain_ref, *refs):
    blocks = lax.axis_size("col")
    block_refs, refs = refs[:blocks], refs[blocks:]
    *weight_refs, own_ref, send_ref, held = refs
    row, col = place_ref[0], place_ref[1]
    for step, ref in enumerate(block_refs):
        index = lax.rem(col - step + blocks, blocks)
        gain = gain_ref[pl.ds(2 * index + lax.rem(row, 2), 1), :]
        held[index] = (ref[...].astype(jnp.float32) * gain).astype(jnp.bfloat16)
    def piece(step, part, start, stop):
        return half_ref(weight_refs, step, part)[:, start:stop]

    width = weight_refs[0].shape[2]
    multiply_pieces(((0, 1),), held, row // 2, piece, width, (own_ref,), (send_ref,))


def project_ffn(place, gain, token_blocks, pieces):
    tokens_two, depth = token_blocks[0].shape
    blocks, count = len(token_blocks), tokens_two // 2
    columns = 2 * pieces[0].shape[2]
    return pl.pallas_call(
        ffn_in_kernel,
        out_shape=(
            jax.ShapeDtypeStruct((count, columns), jnp.float32),
            jax.ShapeDtypeStruct((count, columns), jnp.bfloat16),
        ),
        in_specs=[SMEM] + [VMEM] * (1 + blocks + len(pieces)),
        out_specs=(VMEM, VMEM),
        scratch_shapes=[pltpu.VMEM((blocks, tokens_two, depth), jnp.bfloat16)],
        compiler_params=pltpu.CompilerParams(vmem_limit_bytes=8 << 20),
        cost_estimate=pl.CostEstimate(
            flops=2 * tokens_two * depth * blocks * columns,
            bytes_accessed=2 * depth * blocks * columns,
            transcendentals=0,
        ),
        name="ffn_in",
    )(place, gain, *token_blocks, *pieces)


def columns_kernel(cut, place_ref, own_in_ref, other_in_ref, *refs):
    blocks = lax.axis_size("col")
    *weight_refs, own_ref = refs[: len(refs) - blocks]
    send_refs, held = refs[len(refs) - blocks : -1], refs[-1]
    row, col = place_ref[0], place_ref[1]
    pair = row // 2
    hidden = jnp.concatenate([own_in_ref[...], other_in_ref[...]], axis=0)
    far = len(weight_refs) == blocks + 1
    direct = blocks - 1 if far else blocks
    for step in range(blocks):
        if cut:
            low, high = (
                weight_refs[0][:cut] if step == 0 else half_ref(weight_refs, step, 0)[...],
                weight_refs[0][cut:] if step == 0 else half_ref(weight_refs, step, 1)[...],
            )
            total = jnp.dot(
                hidden[:, :cut], low, preferred_element_type=jnp.float32
            ) + jnp.dot(hidden[:, cut:], high, preferred_element_type=jnp.float32)
        elif step < direct:
            total = jnp.dot(hidden, weight_refs[step][...], preferred_element_type=jnp.float32)
        else:
            half = hidden.shape[1] // 2
            low, high = (ref[...] for ref in weight_refs[direct:])
            total = jnp.dot(
                hidden[:, :half], low, preferred_element_type=jnp.float32
            ) + jnp.dot(hidden[:, half:], high, preferred_element_type=jnp.float32)
        held[lax.rem((pair ^ step) - col + blocks, blocks)] = total
    own_ref[...] = held[0]
    for step in range(1, blocks):
        send_refs[step - 1][...] = held[step].astype(jnp.bfloat16)


def columns(place, own, other, pieces, name, cut=0):
    count, depth = own.shape
    width = pieces[0].shape[-1]
    blocks = lax.axis_size("col")
    return pl.pallas_call(
        functools.partial(columns_kernel, cut),
        out_shape=(
            jax.ShapeDtypeStruct((2 * count, width), jnp.float32),
            *[jax.ShapeDtypeStruct((2 * count, width), jnp.bfloat16)] * (blocks - 1),
        ),
        in_specs=[SMEM] + [VMEM] * (2 + len(pieces)),
        out_specs=tuple([VMEM] * blocks),
        scratch_shapes=[pltpu.VMEM((blocks, 2 * count, width), jnp.float32)],
        compiler_params=pltpu.CompilerParams(vmem_limit_bytes=8 << 20),
        cost_estimate=pl.CostEstimate(
            flops=4 * count * depth * width * blocks,
            bytes_accessed=2 * depth * width * blocks,
            transcendentals=0,
        ),
        name=name,
    )(place, own, other, *pieces)


def summed(own, sends, residual):
    total = own + residual.astype(jnp.float32)
    for step, send in enumerate(sends, 1):
        total = total + shifted(send, step).astype(jnp.float32)
    return total.astype(jnp.bfloat16)


def gathered(block):
    return [block] + [shifted(block, step) for step in range(1, lax.axis_size("col"))]


def square_sums(blocks):
    return sum(jnp.sum(jnp.square(b.astype(jnp.float32)), axis=1) for b in blocks)


def per_device(
    tokens,
    segment_ids,
    bucket_table,
    slot_index,
    gain_attn,
    w_qkv,
    rel_bias,
    w_out,
    gain_ffn,
    w_in,
    w_down,
):
    rows, cols = lax.axis_size("row"), lax.axis_size("col")
    count, width = tokens.shape
    half = width // 2
    features = width * cols
    row, col = lax.axis_index("row"), lax.axis_index("col")
    core = row % 2
    place = jnp.stack([row, col]).astype(jnp.int32)

    qkv_near = near_pieces(w_qkv)
    token_blocks = gathered(tokens)
    kept, given = norm_tokens(place, gain_attn.reshape(cols, width), token_blocks)
    out_near = near_pieces(after(w_out, token_blocks[1]))
    token_block = jnp.concatenate(
        [
            jnp.where(core == 0, tokens[:, :half], tokens[:, half:]),
            other_core(jnp.where(core == 0, tokens[:, half:], tokens[:, :half])),
        ],
        axis=0,
    )
    bias = masked_bias(row, segment_ids, bucket_table, rel_bias, count)
    *qkv_near, kept, given, token_block = lax.optimization_barrier(
        (*qkv_near, kept, given, token_block)
    )
    received = other_core(given)
    qkv_far = relayed(qkv_near, 2, "relay_qkv")
    *out_near, received, bias = lax.optimization_barrier((*out_near, received, bias))
    out_far = relayed(out_near, 0, "relay_out")
    w_in, w_down, *_ = lax.optimization_barrier((w_in, w_down, received))
    cut = w_down.shape[0] * 9 // 20 // 16 * 16
    down_first = first_phase(w_down[:cut], w_down[cut:])
    in_first = first_phase(w_in[0], w_in[1])
    gain_rows = gain_ffn.reshape(rows, -1)
    kept, gain_rows, *out_far = lax.optimization_barrier((kept, gain_rows, *out_far))
    own_q, own_kv, send_q, send_kv = project_qkv(
        place, kept, received, [w_qkv, *qkv_near, *qkv_far]
    )
    other_kv, other_q, *down_first = lax.optimization_barrier(
        (other_core(send_kv), other_core(send_q), *down_first)
    )
    key_value = (own_kv + other_kv).astype(jnp.bfloat16)
    packets = second_phase(w_down, down_first)
    queries = (own_q + other_q).astype(jnp.bfloat16)
    forward = [(i, i + 1) for i in range(rows - 1)]
    backward = [(target, source) for source, target in forward]
    low = lax.ppermute(key_value, "row", forward)
    high = lax.ppermute(key_value, "row", backward)
    low, high, *waited = lax.optimization_barrier((low, high, *in_first, *packets))
    in_first, packets = waited[: len(in_first)], waited[len(in_first) :]
    in_pieces = [w_in, *in_first, *exchanged(second_phase(w_in, in_first))]
    context = attention(queries, low, key_value, high, bias)
    own, *sends = columns(
        place, context, other_core(context), [w_out, *out_near, *out_far], "attention_out"
    )
    stacked = jnp.stack([key_value[:, :width], key_value[:, width:]])
    blocks = stacked.reshape(2, slot_index.shape[1], BLOCK, width)
    kv_cache = jnp.zeros_like(blocks)
    for index in range(slot_index.shape[1]):
        kv_cache = lax.dynamic_update_slice_in_dim(
            kv_cache, blocks[:, index : index + 1], slot_index[0, index], axis=1
        )
    kv_cache = kv_cache.reshape(2, count, width)
    middle, kv_cache = lax.optimization_barrier((summed(own, sends, token_block), kv_cache))

    middle_blocks = gathered(middle)
    squares = square_sums(middle_blocks)
    squares = squares[:count] + other_core(squares[count:])
    scale = lax.rsqrt(squares / features + epsilon)[:, None]
    down_second = exchanged(after_all(packets, middle_blocks[-1]))
    own, send = project_ffn(
        place, gain_rows, middle_blocks, in_pieces
    )
    scale, *down_second = lax.optimization_barrier((scale, *down_second))
    branches = (own + other_core(send).astype(jnp.float32)) * scale
    inner = branches.shape[1] // 2
    hidden = (
        jax.nn.gelu(branches[:, :inner], approximate=True) * branches[:, inner:]
    ).astype(jnp.bfloat16)
    own, *sends = columns(
        place, hidden, other_core(hidden), [w_down, *down_first, *down_second], "ffn_out", cut
    )
    result = summed(own, sends, middle)
    received = other_core(result[count:])
    output = jnp.where(
        core == 0,
        jnp.concatenate([result[:count], received], axis=1),
        jnp.concatenate([received, result[:count]], axis=1),
    )

    return (output, kv_cache)


def solution(mesh):
    return jax.shard_map(
        per_device,
        mesh=mesh,
        in_specs=(
            P("row", "col"),
            P(),
            P(),
            P("row", None),
            P(),
            P(None, "row", "col"),
            P(None, "col"),
            P("col", "row"),
            P(),
            P(None, "row", "col"),
            P("col", "row"),
        ),
        out_specs=(P("row", "col"), P(None, "row", "col")),
        check_vma=False,
    )
```

```python
import functools

import jax
import jax.numpy as jnp
from jax import lax
from jax.experimental import pallas as pl
from jax.experimental.pallas import tpu as pltpu
from jax.sharding import PartitionSpec as P

BLOCK = 128


epsilon = 1e-06
masked_score = -1e30
VMEM = pl.BlockSpec(memory_space=pltpu.VMEM)
SMEM = pl.BlockSpec(memory_space=pltpu.SMEM)


def bias_kernel(row_ref, seg_ref, table_ref, rel_ref, out_ref):
    heads, count, width = out_ref.shape
    rows = seg_ref.shape[0]
    row = row_ref[0]
    table = table_ref[...]
    rel = rel_ref[...]
    by_distance = jnp.zeros((heads, table.shape[1]), jnp.float32)
    for bucket in range(rel.shape[1]):
        by_distance = jnp.where(table == bucket, rel[:, bucket : bucket + 1], by_distance)
    by_distance = jnp.concatenate(
        [by_distance, jnp.zeros((heads, width - table.shape[1]), jnp.float32)], axis=1
    )

    def segment_row(index):
        clipped = jnp.clip(index, 0, rows - 1)
        found = seg_ref[pl.ds(clipped, 1), :].astype(jnp.float32)
        return jnp.where(index == clipped, found, -1.0)

    own = segment_row(row)
    query_seg = jnp.broadcast_to(own, (count, count)).T
    allowed = jnp.concatenate(
        [query_seg == segment_row(row - 1), query_seg == own, query_seg == segment_row(row + 1)],
        axis=1,
    )
    for head in range(heads):
        line = jnp.broadcast_to(by_distance[head : head + 1, :], (count, width))
        shifted = pltpu.roll(line, 1, 1, stride=1, stride_axis=0)
        out_ref[head] = jnp.where(allowed, shifted, masked_score)


def masked_bias(row, segment_ids, bucket_table, rel_bias, count):
    heads = rel_bias.shape[1]
    table = jnp.pad(bucket_table, (0, 1)).reshape(1, 2 * count)
    return pl.pallas_call(
        bias_kernel,
        out_shape=jax.ShapeDtypeStruct((heads, count, 3 * count), jnp.float32),
        in_specs=[SMEM, VMEM, VMEM, VMEM],
        out_specs=VMEM,
        compiler_params=pltpu.CompilerParams(vmem_limit_bytes=8 << 20),
        name="masked_bias",
    )(row.reshape(1), segment_ids.reshape(-1, count), table, rel_bias.T)


def attention_kernel(q_ref, low_ref, own_ref, high_ref, bias_ref, out_ref):
    heads, count, _ = bias_ref.shape
    total_width = q_ref.shape[1]
    width = total_width // heads
    sides = (low_ref, own_ref, high_ref)
    for pair in range(0, heads, 2):
        parts = []
        for head in (pair, pair + 1):
            cut = slice(head * width, (head + 1) * width)
            after_keys = slice(total_width + head * width, total_width + (head + 1) * width)
            query = q_ref[:, cut]
            scores = jnp.concatenate(
                [
                    lax.dot_general(
                        query,
                        ref[:, cut],
                        (((1,), (1,)), ((), ())),
                        preferred_element_type=jnp.float32,
                    )
                    for ref in sides
                ],
                axis=1,
            )
            scores = scores + bias_ref[head]
            top = jnp.max(scores, axis=1, keepdims=True)
            weights = jnp.exp(scores - top)
            denominator = jnp.sum(weights, axis=1, keepdims=True)
            rounded = weights.astype(jnp.bfloat16)
            total = sum(
                jnp.dot(
                    rounded[:, i * count : (i + 1) * count],
                    ref[:, after_keys],
                    preferred_element_type=jnp.float32,
                )
                for i, ref in enumerate(sides)
            )
            parts.append(total / denominator)
        out_ref[:, pair * width : (pair + 2) * width] = jnp.concatenate(parts, axis=1).astype(
            out_ref.dtype
        )


def attention(queries, low, own, high, bias):
    count, span = bias.shape[1:]
    return pl.pallas_call(
        attention_kernel,
        out_shape=jax.ShapeDtypeStruct(queries.shape, jnp.bfloat16),
        in_specs=[VMEM] * 5,
        out_specs=VMEM,
        compiler_params=pltpu.CompilerParams(vmem_limit_bytes=8 << 20),
        cost_estimate=pl.CostEstimate(
            flops=4 * queries.size * span, bytes_accessed=4 * bias.size, transcendentals=bias.size
        ),
        name="attention",
    )(queries, low, own, high, bias)


def exchange(value, axis, partner):
    count = lax.axis_size(axis)
    return lax.ppermute(value, axis, [(i, partner(i) % count) for i in range(count)])


def other_core(value):
    return exchange(value, "row", lambda i: i ^ 1)


def pair_exchange(value, step):
    return exchange(value, "row", lambda i: i ^ (2 * step))


def shifted(value, step):
    return exchange(value, "col", lambda i: i + step)


def after(value, *earlier):
    return lax.optimization_barrier((value, *earlier))[0]


def near_pieces(weight):
    pairs = lax.axis_size("row") // 2
    if pairs == 4:
        return [pair_exchange(weight, 1), pair_exchange(weight, 2)]
    return [pair_exchange(weight, step) for step in range(1, pairs)]


def after_all(values, *earlier):
    return list(lax.optimization_barrier((*values, *earlier))[: len(values)])


def first_hop(weight, *earlier):
    weight = after(weight, *earlier)
    return weight, near_pieces(weight)


def first_phase(low, high):
    pairs = lax.axis_size("row") // 2
    if pairs != 4:
        return [pair_exchange(part, step) for step in range(1, pairs) for part in (low, high)]
    return [pair_exchange(low, 1), pair_exchange(high, 2)]


def packet_kernel(own_ref, low_in, high_in, low_ref, high_ref):
    cut = low_in.shape[0]
    stacked = len(own_ref.shape) == 3
    low_ref[0] = own_ref[0] if stacked else own_ref[:cut]
    high_ref[0] = own_ref[1] if stacked else own_ref[cut:]
    low_ref[1], high_ref[1] = low_in[...], high_in[...]


def second_phase(own, first):
    if len(first) != 2:
        return []
    low, high = pl.pallas_call(
        packet_kernel,
        out_shape=tuple(jax.ShapeDtypeStruct((2, *part.shape), part.dtype) for part in first),
        in_specs=[VMEM] * 3,
        out_specs=(VMEM, VMEM),
        compiler_params=pltpu.CompilerParams(vmem_limit_bytes=8 << 20),
        name="packet",
    )(own, *first)
    return [low, high]


def exchanged(packets):
    return [pair_exchange(packet, step) for packet, step in zip(packets[::-1], (1, 2))]


def half_ref(refs, step, part):
    own, *others = refs
    if step == 0:
        return own.at[part]
    if len(others) != 4:
        return others[2 * (step - 1) + part]
    near_low, side_high, highs, lows = others
    if step == 3:
        return (highs if part else lows).at[1]
    if part == step - 1:
        return near_low if part == 0 else side_high
    return (highs if part else lows).at[0]


def norm_kernel(place_ref, gain_ref, *refs):
    *block_refs, kept_ref, given_ref = refs
    blocks = len(block_refs)
    core, col = lax.rem(place_ref[0], 2), place_ref[1]
    wide = [ref[...].astype(jnp.float32) for ref in block_refs]
    squares = sum(jnp.sum(block * block, axis=1, keepdims=True) for block in wide)
    half = wide[0].shape[1] // 2
    scale = lax.rsqrt(squares / (2 * half * blocks) + epsilon)
    for step, block in enumerate(wide):
        index = lax.rem(col - step + blocks, blocks)
        normed = (block * scale * gain_ref[pl.ds(index, 1), :]).astype(jnp.bfloat16)
        low, high = normed[:, :half], normed[:, half:]
        kept_ref[index] = jnp.where(core == 0, low, high)
        given_ref[index] = jnp.where(core == 0, high, low)


def norm_tokens(place, gain, token_blocks):
    count, width = token_blocks[0].shape
    shape = jax.ShapeDtypeStruct((len(token_blocks), count, width // 2), jnp.bfloat16)
    return pl.pallas_call(
        norm_kernel,
        out_shape=(shape, shape),
        in_specs=[SMEM] + [VMEM] * (1 + len(token_blocks)),
        out_specs=(VMEM, VMEM),
        compiler_params=pltpu.CompilerParams(vmem_limit_bytes=8 << 20),
        name="norm_tokens",
    )(place, gain, *token_blocks)


def multiply_pieces(groups, held, pair, piece, width, own_refs, send_refs):
    blocks, tokens_two, _ = held.shape
    count = tokens_two // 2
    tile = min(256, width, held.shape[2])
    for group, own_ref, send_ref in zip(groups, own_refs, send_refs):
        for place, part in enumerate(group):
            for start in range(0, width, tile):
                stop = min(start + tile, width)
                total = None
                for step in range(blocks):
                    weight = piece(step, part, start, stop)
                    term = jnp.dot(held[pair ^ step], weight, preferred_element_type=jnp.float32)
                    total = term if total is None else total + term
                where = slice(place * width + start, place * width + stop)
                own_ref[:, where] = total[:count]
                send_ref[:, where] = total[count:].astype(send_ref.dtype)


def relay_kernel(axis, low_in, high_in, low_ref, high_ref):
    half = low_ref.shape[axis]
    low_ref[...] = low_in[:half] if axis == 0 else low_in[:, :, :half]
    high_ref[...] = high_in[half:] if axis == 0 else high_in[:, :, half:]


def relayed(near, axis, name):
    if len(near) != 2:
        return []
    dims = list(near[0].shape)
    dims[axis] //= 2
    shape = jax.ShapeDtypeStruct(tuple(dims), near[0].dtype)
    low, high = pl.pallas_call(
        functools.partial(relay_kernel, axis),
        out_shape=(shape, shape),
        in_specs=[VMEM] * 2,
        out_specs=(VMEM, VMEM),
        compiler_params=pltpu.CompilerParams(vmem_limit_bytes=8 << 20),
        name=name,
    )(*near)
    return [pair_exchange(low, 2), pair_exchange(high, 1)]


def qkv_kernel(place_ref, own_in_ref, other_in_ref, *refs):
    *weight_refs, own_q, own_kv, send_q, send_kv, held = refs
    count = own_in_ref.shape[1]
    held[:, :count] = own_in_ref[...]
    held[:, count:] = other_in_ref[...]
    blocks, width = held.shape[0], own_q.shape[1]
    direct = blocks - 1 if len(weight_refs) == blocks + 1 else blocks

    def piece(step, part, start, stop):
        if step < direct:
            return weight_refs[step][part, :, start:stop]
        half = start // (width // 2)
        offset = start - half * (width // 2)
        return weight_refs[direct + half][part, :, offset : offset + stop - start]

    multiply_pieces(
        ((0,), (1, 2)), held, place_ref[0] // 2, piece, width, (own_q, own_kv), (send_q, send_kv)
    )


def project_qkv(place, own, other, pieces):
    blocks, count, depth = own.shape
    width = 2 * depth
    shapes = [jax.ShapeDtypeStruct((count, n * width), jnp.float32) for n in (1, 2)] * 2
    return pl.pallas_call(
        qkv_kernel,
        out_shape=tuple(shapes),
        in_specs=[SMEM] + [VMEM] * (2 + len(pieces)),
        out_specs=tuple([VMEM] * 4),
        scratch_shapes=[pltpu.VMEM((blocks, 2 * count, depth), jnp.bfloat16)],
        compiler_params=pltpu.CompilerParams(vmem_limit_bytes=8 << 20),
        cost_estimate=pl.CostEstimate(
            flops=12 * count * depth * blocks * width,
            bytes_accessed=6 * depth * blocks * width,
            transcendentals=0,
        ),
        name="qkv",
    )(place, own, other, *pieces)


def ffn_in_kernel(place_ref, gain_ref, *refs):
    blocks = lax.axis_size("col")
    block_refs, refs = refs[:blocks], refs[blocks:]
    *weight_refs, own_ref, send_ref, held = refs
    row, col = place_ref[0], place_ref[1]
    for step, ref in enumerate(block_refs):
        index = lax.rem(col - step + blocks, blocks)
        gain = gain_ref[pl.ds(2 * index + lax.rem(row, 2), 1), :]
        held[index] = (ref[...].astype(jnp.float32) * gain).astype(jnp.bfloat16)
    def piece(step, part, start, stop):
        return half_ref(weight_refs, step, part)[:, start:stop]

    width = weight_refs[0].shape[2]
    multiply_pieces(((0, 1),), held, row // 2, piece, width, (own_ref,), (send_ref,))


def project_ffn(place, gain, token_blocks, pieces):
    tokens_two, depth = token_blocks[0].shape
    blocks, count = len(token_blocks), tokens_two // 2
    columns = 2 * pieces[0].shape[2]
    return pl.pallas_call(
        ffn_in_kernel,
        out_shape=(
            jax.ShapeDtypeStruct((count, columns), jnp.float32),
            jax.ShapeDtypeStruct((count, columns), jnp.bfloat16),
        ),
        in_specs=[SMEM] + [VMEM] * (1 + blocks + len(pieces)),
        out_specs=(VMEM, VMEM),
        scratch_shapes=[pltpu.VMEM((blocks, tokens_two, depth), jnp.bfloat16)],
        compiler_params=pltpu.CompilerParams(vmem_limit_bytes=8 << 20),
        cost_estimate=pl.CostEstimate(
            flops=2 * tokens_two * depth * blocks * columns,
            bytes_accessed=2 * depth * blocks * columns,
            transcendentals=0,
        ),
        name="ffn_in",
    )(place, gain, *token_blocks, *pieces)


def columns_kernel(cut, place_ref, own_in_ref, other_in_ref, *refs):
    blocks = lax.axis_size("col")
    *weight_refs, own_ref = refs[: len(refs) - blocks]
    send_refs, held = refs[len(refs) - blocks : -1], refs[-1]
    row, col = place_ref[0], place_ref[1]
    pair = row // 2
    hidden = jnp.concatenate([own_in_ref[...], other_in_ref[...]], axis=0)
    far = len(weight_refs) == blocks + 1
    direct = blocks - 1 if far else blocks
    for step in range(blocks):
        if cut:
            low, high = (
                weight_refs[0][:cut] if step == 0 else half_ref(weight_refs, step, 0)[...],
                weight_refs[0][cut:] if step == 0 else half_ref(weight_refs, step, 1)[...],
            )
            total = jnp.dot(
                hidden[:, :cut], low, preferred_element_type=jnp.float32
            ) + jnp.dot(hidden[:, cut:], high, preferred_element_type=jnp.float32)
        elif step < direct:
            total = jnp.dot(hidden, weight_refs[step][...], preferred_element_type=jnp.float32)
        else:
            half = hidden.shape[1] // 2
            low, high = (ref[...] for ref in weight_refs[direct:])
            total = jnp.dot(
                hidden[:, :half], low, preferred_element_type=jnp.float32
            ) + jnp.dot(hidden[:, half:], high, preferred_element_type=jnp.float32)
        held[lax.rem((pair ^ step) - col + blocks, blocks)] = total
    own_ref[...] = held[0]
    for step in range(1, blocks):
        send_refs[step - 1][...] = held[step].astype(jnp.bfloat16)


def columns(place, own, other, pieces, name, cut=0):
    count, depth = own.shape
    width = pieces[0].shape[-1]
    blocks = lax.axis_size("col")
    return pl.pallas_call(
        functools.partial(columns_kernel, cut),
        out_shape=(
            jax.ShapeDtypeStruct((2 * count, width), jnp.float32),
            *[jax.ShapeDtypeStruct((2 * count, width), jnp.bfloat16)] * (blocks - 1),
        ),
        in_specs=[SMEM] + [VMEM] * (2 + len(pieces)),
        out_specs=tuple([VMEM] * blocks),
        scratch_shapes=[pltpu.VMEM((blocks, 2 * count, width), jnp.float32)],
        compiler_params=pltpu.CompilerParams(vmem_limit_bytes=8 << 20),
        cost_estimate=pl.CostEstimate(
            flops=4 * count * depth * width * blocks,
            bytes_accessed=2 * depth * width * blocks,
            transcendentals=0,
        ),
        name=name,
    )(place, own, other, *pieces)


def summed(own, sends, residual):
    total = own + residual.astype(jnp.float32)
    for step, send in enumerate(sends, 1):
        total = total + shifted(send, step).astype(jnp.float32)
    return total.astype(jnp.bfloat16)


def gathered(block):
    return [block] + [shifted(block, step) for step in range(1, lax.axis_size("col"))]


def square_sums(blocks):
    return sum(jnp.sum(jnp.square(b.astype(jnp.float32)), axis=1) for b in blocks)


def per_device(
    tokens,
    segment_ids,
    bucket_table,
    slot_index,
    gain_attn,
    w_qkv,
    rel_bias,
    w_out,
    gain_ffn,
    w_in,
    w_down,
):
    rows, cols = lax.axis_size("row"), lax.axis_size("col")
    count, width = tokens.shape
    half = width // 2
    features = width * cols
    row, col = lax.axis_index("row"), lax.axis_index("col")
    core = row % 2
    place = jnp.stack([row, col]).astype(jnp.int32)

    qkv_near = near_pieces(w_qkv)
    token_blocks = gathered(tokens)
    kept, given = norm_tokens(place, gain_attn.reshape(cols, width), token_blocks)
    out_near = near_pieces(after(w_out, token_blocks[1]))
    token_block = jnp.concatenate(
        [
            jnp.where(core == 0, tokens[:, :half], tokens[:, half:]),
            other_core(jnp.where(core == 0, tokens[:, half:], tokens[:, :half])),
        ],
        axis=0,
    )
    bias = masked_bias(row, segment_ids, bucket_table, rel_bias, count)
    *qkv_near, kept, given, token_block = lax.optimization_barrier(
        (*qkv_near, kept, given, token_block)
    )
    received = other_core(given)
    qkv_far = relayed(qkv_near, 2, "relay_qkv")
    *out_near, received, bias = lax.optimization_barrier((*out_near, received, bias))
    out_far = relayed(out_near, 0, "relay_out")
    w_in, w_down, *_ = lax.optimization_barrier((w_in, w_down, received))
    cut = w_down.shape[0] * 9 // 20 // 16 * 16
    down_first = first_phase(w_down[:cut], w_down[cut:])
    in_first = first_phase(w_in[0], w_in[1])
    gain_rows = gain_ffn.reshape(rows, -1)
    kept, gain_rows, *out_far = lax.optimization_barrier((kept, gain_rows, *out_far))
    own_q, own_kv, send_q, send_kv = project_qkv(
        place, kept, received, [w_qkv, *qkv_near, *qkv_far]
    )
    other_kv, other_q, *down_first = lax.optimization_barrier(
        (other_core(send_kv), other_core(send_q), *down_first)
    )
    key_value = (own_kv + other_kv).astype(jnp.bfloat16)
    packets = second_phase(w_down, down_first)
    queries = (own_q + other_q).astype(jnp.bfloat16)
    forward = [(i, i + 1) for i in range(rows - 1)]
    backward = [(target, source) for source, target in forward]
    low = lax.ppermute(key_value, "row", forward)
    high = lax.ppermute(key_value, "row", backward)
    low, high, *waited = lax.optimization_barrier((low, high, *in_first, *packets))
    in_first, packets = waited[: len(in_first)], waited[len(in_first) :]
    in_pieces = [w_in, *in_first, *exchanged(second_phase(w_in, in_first))]
    context = attention(queries, low, key_value, high, bias)
    own, *sends = columns(
        place, context, other_core(context), [w_out, *out_near, *out_far], "attention_out"
    )
    stacked = jnp.stack([key_value[:, :width], key_value[:, width:]])
    blocks = stacked.reshape(2, slot_index.shape[1], BLOCK, width)
    kv_cache = jnp.zeros_like(blocks)
    for index in range(slot_index.shape[1]):
        kv_cache = lax.dynamic_update_slice_in_dim(
            kv_cache, blocks[:, index : index + 1], slot_index[0, index], axis=1
        )
    kv_cache = kv_cache.reshape(2, count, width)
    middle, kv_cache = lax.optimization_barrier((summed(own, sends, token_block), kv_cache))

    middle_blocks = gathered(middle)
    squares = square_sums(middle_blocks)
    squares = squares[:count] + other_core(squares[count:])
    scale = lax.rsqrt(squares / features + epsilon)[:, None]
    down_second = exchanged(after_all(packets, middle_blocks[-1]))
    own, send = project_ffn(
        place, gain_rows, middle_blocks, in_pieces
    )
    branches = (own + other_core(send).astype(jnp.float32)) * scale
    inner = branches.shape[1] // 2
    hidden = (
        jax.nn.gelu(branches[:, :inner], approximate=True) * branches[:, inner:]
    ).astype(jnp.bfloat16)
    hidden, *down_second = lax.optimization_barrier((hidden, *down_second))
    own, *sends = columns(
        place, hidden, other_core(hidden), [w_down, *down_first, *down_second], "ffn_out", cut
    )
    result = summed(own, sends, middle)
    received = other_core(result[count:])
    output = jnp.where(
        core == 0,
        jnp.concatenate([result[:count], received], axis=1),
        jnp.concatenate([received, result[:count]], axis=1),
    )

    return (output, kv_cache)


def solution(mesh):
    return jax.shard_map(
        per_device,
        mesh=mesh,
        in_specs=(
            P("row", "col"),
            P(),
            P(),
            P("row", None),
            P(),
            P(None, "row", "col"),
            P(None, "col"),
            P("col", "row"),
            P(),
            P(None, "row", "col"),
            P("col", "row"),
        ),
        out_specs=(P("row", "col"), P(None, "row", "col")),
        check_vma=False,
    )
```
